512 devices in a mesh: seq: 64 (over z, y), tp: 8 (over x, core).
Axes of the slice: x: 4, y: 4, z: 16, core: 2. Of those that a mesh axis runs over, the one named last changes fastest.
Arguments:
- features: float32 [3, 4096, 16384], P(None, 'tp', 'seq'), may hold values from -6 to 6
- short_filter: float32 [3, 256, 7], P(None, 'tp'), may hold values from -2 to 2
- medium_filter: float32 [3, 256, 128], P(None, 'tp'), may hold values from -0.5 to 0.5
- rates: float32 [256, 16], P('tp'), as said below
- residues: float32 [256, 16], P('tp'), may hold values from -1.5 to 1.5
- skip_gain: float32 [4096], P('tp'), may hold values from -4 to 4
- out_weight: bfloat16 [2048, 4096], P(None, 'tp'), may hold values from -0.125 to 0.125
Outputs:
- mixed: float32 [2048, 16384], P('tp', 'seq')
The draws below stay inside these ranges and needn't reach their ends.
Inputs may be any that keep to these rules, and one draw needn't show every extreme that they name: `rates`: every rate lies between 1 / 163840 and 1 / 20.
All inputs are finite; a program needn't handle non-finite values.
Results may differ from the reference program's by a relative error of at most 0.0029.
Values sent between devices are 32-bit elements; how exact they have to be, the bound alone decides.
A program may use at most 128 MiB of HBM per device.

```python
import math
import jax
import jax.numpy as jnp
from jax import lax

D = 4096
D_OUT = 2048
GROUP = 16
SHORT = 7
MEDIUM = 128
ORDER = 16
T_DEV = 256
TOKENS = 16384


def draw_rates(key, part):
    key_class, key_level = jax.random.split(jax.random.fold_in(key, 17), 2)
    shape = (D // GROUP, ORDER)
    picker = jax.random.uniform(key_class, shape, jnp.float32)
    level = jax.random.uniform(key_level, shape, jnp.float32)
    slow_rate = jnp.exp(math.log(0.1 / TOKENS) + level * math.log(20.0))
    fast_rate = jnp.exp(math.log(0.02) + level * math.log(2.5))
    middle_rate = jnp.exp(math.log(0.25 / T_DEV) + level * math.log(16.0))
    chosen = jnp.where(picker < 0.3, fast_rate, jnp.where(picker < 0.5, middle_rate, slow_rate))
    return chosen.astype(jnp.float32)


def spiked(values, stream_key, source, target, parts, factor):
    owner, partner = [(jnp.arange(values.shape[axis_at]) // (values.shape[axis_at] // parts)).reshape([-1 if axis == axis_at else 1 for axis in range(values.ndim)]) for axis_at in (source, target)]
    chosen = jax.random.permutation(stream_key, parts)[partner]
    strong = (owner == chosen) | (owner == (partner + parts // 2) % parts)
    return jnp.where(strong, factor * values, values)


def block_levels(rng, dims, cuts, low, top_value):
    def one(dim, parts):
        steps = jax.random.uniform(jax.random.fold_in(jax.random.fold_in(rng, 6), dim), (parts,), jnp.float32, low / len(cuts), top_value / len(cuts))
        return jnp.repeat(jnp.exp(steps), dims[dim] // parts).reshape((-1,) + (1,) * (len(dims) - dim - 1))

    loudness = one(*cuts[0])
    for cut in cuts[1:]:
        loudness = loudness * one(*cut)
    return loudness


def bell_draw(stream_key, extent, scale, reach, pieces=(), kind=jnp.bfloat16):
    values = jax.random.normal(stream_key, extent, jnp.float32) * scale
    if len(pieces) > 0:
        values = block_levels(stream_key, extent, pieces, -0.22, 0.18) * values
    return jnp.clip(values, min=-reach, max=reach).astype(kind)


def noise_with(stream_key, extent, spread, bound, shards, heavy, kind=jnp.bfloat16):
    array = spread * jax.random.normal(stream_key, extent, jnp.float32)
    if shards:
        array = array * block_levels(stream_key, extent, shards, -0.22, 0.18)
    return jnp.clip(spiked(array, jax.random.fold_in(stream_key, 3), *heavy), -bound, bound).astype(kind)


def setup_inputs(seed: int = 0) -> dict:
    streams_of = jax.random.split(jax.random.key(seed), 8)
    return {
        "features": bell_draw(streams_of[0], (3, D, TOKENS), 1.0, 6.0, ((1, 8), (2, 64)), jnp.float32),
        "short_filter": bell_draw(streams_of[1], (3, D // GROUP, SHORT), SHORT ** -0.5, 2.0, ((1, 8),), jnp.float32),
        "medium_filter": bell_draw(streams_of[2], (3, D // GROUP, MEDIUM), MEDIUM ** -0.5, 0.5, ((1, 8),), jnp.float32),
        "rates": draw_rates(jax.random.fold_in(streams_of[7], 71), 0),
        "residues": bell_draw(streams_of[4], (D // GROUP, ORDER), 0.25, 1.5, ((0, 8),), jnp.float32),
        "skip_gain": bell_draw(streams_of[5], (D,), 1.0, 4.0, ((0, 8),), jnp.float32),
        "out_weight": noise_with(streams_of[6], (D_OUT, D), D ** -0.5, 0.125, ((1, 8),), (1, 0, 8, 2.0)),
    }


def short_conv(extended, filters, length):
    coeffs = jnp.repeat(filters, GROUP, axis=1)
    summed = jnp.zeros(extended.shape[:-1] + (length,), extended.dtype)
    for offset in range(SHORT):
        first = SHORT - 1 - offset
        summed = summed + coeffs[:, :, offset:offset + 1] * extended[:, :, first:first + length]
    return summed

def medium_matrix(coeffs):
    block_len = coeffs.shape[0]
    pattern = jnp.concatenate([coeffs[::-1], jnp.zeros((block_len,), coeffs.dtype)])
    return jnp.tile(pattern, block_len)[:block_len * (2 * block_len - 1)].reshape(block_len, 2 * block_len - 1)

def medium_branch(operands):
    extended, coeffs = operands
    block_len = coeffs.shape[1]
    channels = extended.shape[0]
    groups = coeffs.shape[0]
    length = extended.shape[1] - (block_len - 1)
    block_count = length // block_len
    padded = jnp.concatenate([jnp.zeros((channels, 1), extended.dtype), extended], axis=1)
    blocks = padded.reshape(channels, block_count + 1, block_len)
    windows = jnp.concatenate([blocks[:, :-1], blocks[:, 1:]], axis=2)[:, :, 1:]
    windows = windows.reshape(groups, channels // groups, block_count, 2 * block_len - 1)
    matrices = jax.vmap(medium_matrix)(coeffs)
    result = jnp.einsum('gcbs,gts->gcbt', windows, matrices, precision=lax.Precision.HIGHEST)
    return result.reshape(channels, length)

def long_matrix(kernel):
    block_len = kernel.shape[0]
    pattern = jnp.concatenate([kernel[0:1], jnp.zeros((block_len,), kernel.dtype), kernel[1:][::-1]])
    full = jnp.tile(pattern, block_len)[:block_len * (2 * block_len - 1)].reshape(block_len, 2 * block_len - 1)
    return full[:, :block_len]

def modal_tables(rates, residues, block_len):
    steps_axis = jnp.arange(block_len).astype(rates.dtype)
    weight = residues * jnp.sqrt(-jnp.expm1(-2.0 * rates))
    decays = jnp.exp(-rates[:, :, None] * steps_axis)
    kernel = jnp.einsum('gn,gnt->gt', weight, decays, precision=lax.Precision.HIGHEST)
    readout = weight[:, :, None] * jnp.exp(-rates[:, :, None] * (steps_axis + 1.0))
    ending = decays[:, :, ::-1]
    return (kernel, readout, ending)

def long_conv(product, rates, residues):
    block_len = MEDIUM
    groups = rates.shape[0]
    kernel, readout, ending = modal_tables(rates, residues, block_len)
    matrices = jax.vmap(long_matrix)(kernel)
    block_count = TOKENS // block_len
    blocks = product.reshape(groups, GROUP, block_count, block_len).transpose(2, 0, 1, 3)
    step_decay = jnp.exp(-rates * block_len)

    def advance(states, block):
        inside = jnp.einsum('gcs,gts->gct', block, matrices, precision=lax.Precision.HIGHEST)
        carried = jnp.einsum('gcn,gnt->gct', states, readout, precision=lax.Precision.HIGHEST)
        finals = jnp.einsum('gcs,gns->gcn', block, ending, precision=lax.Precision.HIGHEST)
        return (step_decay[:, None, :] * states + finals, inside + carried)
    start_states = jnp.zeros((groups, GROUP, ORDER), product.dtype)
    unused, outputs = lax.scan(advance, start_states, blocks)
    return outputs.transpose(1, 2, 0, 3).reshape(groups * GROUP, TOKENS)

def reference(features, short_filter, medium_filter, rates, residues, skip_gain, out_weight):
    padded = jnp.pad(features, ((0, 0), (0, 0), (SHORT - 1, 0)))
    shorted = short_conv(padded, short_filter, TOKENS)
    extended = jnp.pad(shorted, ((0, 0), (0, 0), (MEDIUM - 1, 0)))
    mediated = lax.map(medium_branch, (extended, medium_filter))
    product = mediated[1] * mediated[2]
    longed = long_conv(product, rates, residues) + skip_gain[:, None] * product
    gated = (mediated[0] * longed).astype(jnp.bfloat16)
    gated = lax.optimization_barrier(gated)
    return jnp.dot(out_weight.astype(jnp.float32), gated.astype(jnp.float32), precision=lax.Precision.HIGHEST)
```

```python
import functools

import jax
import jax.numpy as jnp
from jax import lax
from jax.experimental import pallas as pl
from jax.experimental.pallas import tpu as pltpu
from jax.sharding import PartitionSpec as P

GROUP = 16
SHORT = 7
MEDIUM = 128
ORDER = 16
LANES = 128


def split(x):
    high = x.astype(jnp.bfloat16)
    return high, (x - high.astype(jnp.float32)).astype(jnp.bfloat16)


def dot_split(left, right, dims):
    a_high, a_low = left
    b_high, b_low = right
    one = functools.partial(
        lax.dot_general, dimension_numbers=(dims, ((), ())), preferred_element_type=jnp.float32
    )
    return one(a_high, b_high) + (one(a_high, b_low) + one(a_low, b_high))


NN = ((1,), (0,))
NT = ((1,), (1,))


def iota(shape, axis):
    return lax.broadcasted_iota(jnp.int32, shape, axis)


def filter_tables(short_ref, medium_ref, taps_ref):
    medium = medium_ref[...]
    wide = jnp.concatenate([medium, jnp.zeros_like(medium)], axis=1)
    short = short_ref[...]
    total = short[:, 0:1] * wide
    for j in range(1, SHORT):
        total = total + short[:, j : j + 1] * pltpu.roll(wide, j, 1)
    taps_ref[...] = total


def modal_tables(rates_ref, weight_ref, rate_rows_ref, weight_rows_ref, kernel_ref, ending_ref, readout_ref):
    length = kernel_ref.shape[1]
    steps = iota((1, length), 1).astype(jnp.float32)
    rates, weight = rates_ref[...], weight_ref[...]
    total = weight[:, 0:1] * jnp.exp(-rates[:, 0:1] * steps)
    for n in range(1, ORDER):
        total = total + weight[:, n : n + 1] * jnp.exp(-rates[:, n : n + 1] * steps)
    kernel_ref[...] = total
    rate_rows = rate_rows_ref[...]
    ending_ref[...] = jnp.exp(-rate_rows * (length - 1.0 - steps))
    readout_ref[...] = weight_rows_ref[...] * jnp.exp(-rate_rows * (steps + 1.0))


def toeplitz(row, rows):
    return pltpu.roll(jnp.broadcast_to(row, (rows, row.shape[1])), 0, 1, stride=1, stride_axis=0)


def filter_group(extra, halo, own, taps_row):
    rolled = toeplitz(taps_row, LANES)
    near, middle = rolled[:, :LANES], rolled[:, LANES:]
    causal = iota((LANES, LANES), 1) >= iota((LANES, LANES), 0)
    matrix = jnp.concatenate(
        [jnp.where(causal, 0.0, near), middle, jnp.where(causal, near, 0.0)], axis=0
    )
    tiles = [extra, halo, own[:, :LANES], own[:, LANES:]]
    windows = jnp.concatenate(
        [jnp.concatenate(tiles[0:3], axis=1), jnp.concatenate(tiles[1:4], axis=1)], axis=0
    )
    result = dot_split(split(windows), split(matrix), NN)
    return jnp.concatenate([result[:GROUP], result[GROUP:]], axis=1)


def mix_kernel(
    features_ref, halo_ref, extra_ref, short_ref, medium_ref, rates_ref, weight_ref,
    rate_rows_ref, weight_rows_ref, gain_ref,
    query_ref, base_ref, state_ref, readout_ref,
    taps_ref, kernel_ref, ending_ref, product_ref,
):
    groups, length = kernel_ref.shape
    filter_tables(short_ref, medium_ref, taps_ref)
    modal_tables(rates_ref, weight_ref, rate_rows_ref, weight_rows_ref, kernel_ref, ending_ref, readout_ref)

    def group_step(g, carry):
        rows = pl.ds(pl.multiple_of(g * GROUP, GROUP), GROUP)
        done = [
            filter_group(
                extra_ref[i, rows, :], halo_ref[i, rows, :], features_ref[i, rows, :],
                taps_ref[pl.ds(i * groups + g, 1), :],
            )
            for i in range(3)
        ]
        product = done[1] * done[2]
        query_ref[rows, :] = done[0]
        product_ref[rows, :] = product
        rolled = toeplitz(kernel_ref[pl.ds(g, 1), :], length)
        causal = iota((length, length), 1) >= iota((length, length), 0)
        inside = dot_split(split(product), split(jnp.where(causal, rolled, 0.0)), NN)
        base_ref[rows, :] = inside + gain_ref[rows, :] * product
        return carry

    lax.fori_loop(0, groups, group_step, 0)
    same = iota((LANES, LANES), 0) // ORDER == iota((LANES, LANES), 1) // GROUP
    for block in range(product_ref.shape[0] // LANES):
        rows = slice(block * LANES, (block + 1) * LANES)
        full = dot_split(split(ending_ref[rows, :]), split(product_ref[rows, :]), NT)
        full = jnp.where(same, full, 0.0)
        total = full[0:ORDER]
        for k in range(1, LANES // ORDER):
            total = total + full[k * ORDER : (k + 1) * ORDER]
        state_ref[:, rows] = total


def finish_kernel(query_ref, base_ref, incoming_ref, readout_ref, weight_ref, out_ref, gated_ref):
    same = iota((LANES, LANES), 1) // ORDER == iota((LANES, LANES), 0) // GROUP
    for block in range(query_ref.shape[0] // LANES):
        rows = slice(block * LANES, (block + 1) * LANES)
        across = jnp.transpose(incoming_ref[:, rows])
        spread = jnp.where(same, jnp.concatenate([across] * (LANES // ORDER), axis=1), 0.0)
        carried = dot_split(split(spread), split(readout_ref[rows, :]), NN)
        gated_ref[rows, :] = (query_ref[rows, :] * (base_ref[rows, :] + carried)).astype(jnp.bfloat16)
    gated = gated_ref[...]
    step = 256

    def rows_step(k, carry):
        rows = pl.ds(pl.multiple_of(k * step, step), step)
        out_ref[rows, :] = jnp.dot(weight_ref[rows, :], gated, preferred_element_type=jnp.float32)
        return carry

    lax.fori_loop(0, out_ref.shape[0] // step, rows_step, 0)


def passed_along(block, axis):
    devices = lax.axis_size(axis)
    return lax.ppermute(block, axis, [(i, i + 1) for i in range(devices - 1)])


def vmem():
    return pl.BlockSpec(memory_space=pltpu.VMEM)


def per_device(features, short_filter, medium_filter, rates, residues, skip_gain, out_weight):
    channels, length = features.shape[1:]
    groups = rates.shape[0]
    f32 = jnp.float32
    halo = passed_along(features[:, :, length - LANES :], "seq")
    extra = passed_along(features[:, :, length - LANES - 8 : length - LANES], "seq")
    extra = jnp.pad(extra, ((0, 0), (0, 0), (LANES - 8, 0)))
    weight = residues * jnp.sqrt(-jnp.expm1(-2.0 * rates))
    query, base, state, readout = pl.pallas_call(
        mix_kernel,
        out_shape=(
            jax.ShapeDtypeStruct((channels, length), f32),
            jax.ShapeDtypeStruct((channels, length), f32),
            jax.ShapeDtypeStruct((ORDER, channels), f32),
            jax.ShapeDtypeStruct((groups * ORDER, length), f32),
        ),
        in_specs=[vmem()] * 10,
        out_specs=(vmem(),) * 4,
        scratch_shapes=[
            pltpu.VMEM((3 * groups, length), f32),
            pltpu.VMEM((groups, length), f32),
            pltpu.VMEM((groups * ORDER, length), f32),
            pltpu.VMEM((channels, length), f32),
        ],
        compiler_params=pltpu.CompilerParams(vmem_limit_bytes=48 * 1024 * 1024),
    )(
        features, halo, extra, short_filter.reshape(3 * groups, SHORT), medium_filter.reshape(3 * groups, MEDIUM),
        rates, weight, rates.reshape(-1, 1), weight.reshape(-1, 1), skip_gain[:, None],
    )
    gathered = lax.all_gather(state, "seq")
    count, mine = lax.axis_size("seq"), lax.axis_index("seq")
    place = jnp.arange(count)
    gap = jnp.maximum(mine - 1 - place, 0).astype(f32)
    rates_wide = jnp.repeat(rates.T, GROUP, axis=1)
    decay = jnp.exp(-rates_wide[None] * (length * gap)[:, None, None])
    incoming = jnp.sum(jnp.where((place < mine)[:, None, None], decay * gathered, 0.0), axis=0)
    partial = pl.pallas_call(
        finish_kernel,
        out_shape=jax.ShapeDtypeStruct((out_weight.shape[0], length), f32),
        in_specs=[vmem()] * 5,
        out_specs=vmem(),
        scratch_shapes=[pltpu.VMEM((channels, length), jnp.bfloat16)],
        compiler_params=pltpu.CompilerParams(vmem_limit_bytes=48 * 1024 * 1024),
    )(query, base, incoming, readout, out_weight)
    return lax.psum_scatter(partial, "tp", scatter_dimension=0, tiled=True)


def solution(mesh):
    in_specs = (
        P(None, "tp", "seq"),
        P(None, "tp", None),
        P(None, "tp", None),
        P("tp", None),
        P("tp", None),
        P("tp"),
        P(None, "tp"),
    )
    out_specs = P("tp", "seq")
    return jax.shard_map(
        per_device, mesh=mesh, in_specs=in_specs, out_specs=out_specs, check_vma=False
    )
```

```python
import functools

import jax
import jax.numpy as jnp
from jax import lax
from jax.experimental import pallas as pl
from jax.experimental.pallas import tpu as pltpu
from jax.sharding import PartitionSpec as P

GROUP = 16
SHORT = 7
MEDIUM = 128
ORDER = 16
LANES = 128
ROW = 4
RING = 4


def split(x):
    high = x.astype(jnp.bfloat16)
    return high, (x - high.astype(jnp.float32)).astype(jnp.bfloat16)


def dot_split(left, right, dims):
    a_high, a_low = left
    b_high, b_low = right
    one = functools.partial(
        lax.dot_general, dimension_numbers=(dims, ((), ())), preferred_element_type=jnp.float32
    )
    return one(a_high, b_high) + (one(a_high, b_low) + one(a_low, b_high))


NN = ((1,), (0,))
NT = ((1,), (1,))


def iota(shape, axis):
    return lax.broadcasted_iota(jnp.int32, shape, axis)


def filter_tables(short_ref, medium_ref, taps_ref):
    medium = medium_ref[...]
    wide = jnp.concatenate([medium, jnp.zeros_like(medium)], axis=1)
    short = short_ref[...]
    total = short[:, 0:1] * wide
    for j in range(1, SHORT):
        total = total + short[:, j : j + 1] * pltpu.roll(wide, j, 1)
    taps_ref[...] = total


def modal_tables(rates_ref, weight_ref, rate_rows_ref, weight_rows_ref, kernel_ref, ending_ref, readout_ref):
    length = kernel_ref.shape[1]
    steps = iota((1, length), 1).astype(jnp.float32)
    rates, weight = rates_ref[...], weight_ref[...]
    total = weight[:, 0:1] * jnp.exp(-rates[:, 0:1] * steps)
    for n in range(1, ORDER):
        total = total + weight[:, n : n + 1] * jnp.exp(-rates[:, n : n + 1] * steps)
    kernel_ref[...] = total
    rate_rows = rate_rows_ref[...]
    ending_ref[...] = jnp.exp(-rate_rows * (length - 1.0 - steps))
    readout_ref[...] = weight_rows_ref[...] * jnp.exp(-rate_rows * (steps + 1.0))


def toeplitz(row, rows):
    return pltpu.roll(jnp.broadcast_to(row, (rows, row.shape[1])), 0, 1, stride=1, stride_axis=0)


def filter_group(extra, halo, own, taps_row):
    rolled = toeplitz(taps_row, LANES)
    near, middle = rolled[:, :LANES], rolled[:, LANES:]
    causal = iota((LANES, LANES), 1) >= iota((LANES, LANES), 0)
    matrix = jnp.concatenate(
        [jnp.where(causal, 0.0, near), middle, jnp.where(causal, near, 0.0)], axis=0
    )
    tiles = [extra, halo, own[:, :LANES], own[:, LANES:]]
    windows = jnp.concatenate(
        [jnp.concatenate(tiles[0:3], axis=1), jnp.concatenate(tiles[1:4], axis=1)], axis=0
    )
    result = dot_split(split(windows), split(matrix), NN)
    return jnp.concatenate([result[:GROUP], result[GROUP:]], axis=1)


def wrapped(index, count):
    return lax.rem(index + count, count)


def layer_kernel(
    features_ref, short_ref, medium_ref, rates_ref, weight_ref, rate_rows_ref, weight_rows_ref,
    rate_blocks_ref, gain_ref, out_weight_ref,
    out_ref,
    halo_ref, packed_ref, extra_ref, taps_ref, kernel_ref, ending_ref, readout_ref,
    product_ref, query_ref, base_ref, gated_ref,
    state_ref, row_states_ref, total_ref, totals_ref, start_ref,
    given_ref, mine_ref, pair_ref, relay_ref, last_ref,
    halo_sems, row_sems, column_sems, start_sems, pair_sems, ring_sems,
):
    groups, length = kernel_ref.shape
    channels = product_ref.shape[0]
    blocks = channels // LANES
    count = lax.axis_size("seq")
    column = count // ROW
    seq, tp = lax.axis_index("seq"), lax.axis_index("tp")
    z, y = seq // ROW, lax.rem(seq, ROW)
    x, core = tp // 2, lax.rem(tp, 2)
    at_row = lambda k: (z * ROW + wrapped(y + k, ROW), tp)
    at_column = lambda k: (wrapped(z + k, column) * ROW + y, tp)
    at_ring = lambda k: (seq, wrapped(x + k, RING) * 2 + core)
    following, before = (wrapped(seq + 1, count), tp), (wrapped(seq - 1, count), tp)
    partner = (seq, x * 2 + 1 - core)

    def remote(source, target, sems, device):
        return pltpu.make_async_remote_copy(
            src_ref=source, dst_ref=target, send_sem=sems.at[0], recv_sem=sems.at[1],
            device_id=device, device_id_type=pl.DeviceIdType.MESH,
        )

    barrier = pltpu.get_barrier_semaphore()
    peers = [following, before, partner, at_ring(1), at_ring(-1)]
    peers += [at_row(k) for k in range(1, ROW)] + [at_column(k) for k in range(1, column)]
    for peer in peers:
        pl.semaphore_signal(barrier, inc=1, device_id=peer, device_id_type=pl.DeviceIdType.MESH)
    lane = iota((32, LANES), 1) // 8
    for i in range(3):
        packed = jnp.zeros((32, LANES), jnp.float32)
        for p in range(channels // 32):
            moved = pltpu.roll(features_ref[i, 32 * p : 32 * p + 32, 0:LANES], (8 * p + 8) % LANES, 1)
            packed = jnp.where(lane == p, moved, packed)
        packed_ref[i] = packed
    pl.semaphore_wait(barrier, len(peers))

    halo_copies = [
        remote(features_ref.at[i, :, pl.ds(length - LANES, LANES)], halo_ref.at[i], halo_sems.at[i], following)
        for i in range(3)
    ]
    extra_copy = remote(packed_ref, extra_ref, halo_sems.at[3], following)
    extra_copy.start()
    for i in (1, 2, 0):
        halo_copies[i].start()

    filter_tables(short_ref, medium_ref, taps_ref)
    modal_tables(rates_ref, weight_ref, rate_rows_ref, weight_rows_ref, kernel_ref, ending_ref, readout_ref)
    inner = seq > 0

    def branch(i, g):
        rows = pl.ds(pl.multiple_of(g * GROUP, GROUP), GROUP)
        packed = extra_ref[i, pl.ds(pl.multiple_of(lax.rem(g, 2) * GROUP, GROUP), GROUP), :]
        extra = pltpu.roll(packed, LANES - 8 - 8 * (g // 2), 1)
        zero = jnp.zeros((GROUP, LANES), jnp.float32)
        return filter_group(
            jnp.where(inner, extra, zero), jnp.where(inner, halo_ref[i, rows, :], zero),
            features_ref[i, rows, :], taps_ref[pl.ds(i * groups + g, 1), :],
        )

    def product_step(g, carry):
        rows = pl.ds(pl.multiple_of(g * GROUP, GROUP), GROUP)
        product = branch(1, g) * branch(2, g)
        product_ref[rows, :] = product
        rolled = toeplitz(kernel_ref[pl.ds(g, 1), :], length)
        causal = iota((length, length), 1) >= iota((length, length), 0)
        inside = dot_split(split(product), split(jnp.where(causal, rolled, 0.0)), NN)
        base_ref[rows, :] = inside + gain_ref[rows, :] * product
        return carry

    def query_step(g, carry):
        rows = pl.ds(pl.multiple_of(g * GROUP, GROUP), GROUP)
        query_ref[rows, :] = branch(0, g)
        return carry

    extra_copy.wait_recv()
    halo_copies[1].wait_recv()
    halo_copies[2].wait_recv()
    lax.fori_loop(0, groups, product_step, 0)

    same = iota((LANES, LANES), 0) // ORDER == iota((LANES, LANES), 1) // GROUP
    for b in range(blocks):
        rows = slice(b * LANES, (b + 1) * LANES)
        full = dot_split(split(ending_ref[rows, :]), split(product_ref[rows, :]), NT)
        full = jnp.where(same, full, 0.0)
        total = full[0:ORDER]
        for k in range(1, LANES // ORDER):
            total = total + full[k * ORDER : (k + 1) * ORDER]
        state_ref[b] = total
    row_copies = [
        remote(state_ref, row_states_ref.at[k - 1], row_sems.at[k - 1], at_row(k)) for k in range(1, ROW)
    ]
    for copy in row_copies:
        copy.start()

    halo_copies[0].wait_recv()
    lax.fori_loop(0, groups // 2, query_step, 0)

    for copy in row_copies:
        copy.wait_recv()
    rates = rate_blocks_ref[...]
    decay = lambda rates, steps: jnp.exp(-rates * (float(length) * steps))
    as_float = lambda value: lax.convert_element_type(value, jnp.float32)
    row_start = jnp.zeros(rates.shape, jnp.float32)
    row_total = decay(rates, as_float(ROW - 1 - y)) * state_ref[...]
    for k in range(1, ROW):
        state = row_states_ref[k - 1]
        row_start = row_start + jnp.where(k <= y, decay(rates, k - 1.0) * state, 0.0)
        row_total = row_total + decay(rates, as_float(ROW - 1 - wrapped(y - k, ROW))) * state
    total_ref[...] = row_total
    column_copies = [
        remote(total_ref.at[y], totals_ref.at[k - 1], column_sems.at[k - 1], at_column(k))
        for k in range(1, column)
    ]
    for copy in column_copies:
        copy.start()

    lax.fori_loop(groups // 2, groups, query_step, 0)

    for copy in column_copies:
        copy.wait_recv()
    quarter = rate_blocks_ref[y]
    start = jnp.zeros(quarter.shape, jnp.float32)
    for k in range(1, column):
        start = start + jnp.where(k <= z, decay(quarter, float(ROW * (k - 1))) * totals_ref[k - 1], 0.0)
    start_ref[y] = start
    start_copies = [
        remote(start_ref.at[y], start_ref.at[y], start_sems.at[k - 1], at_row(k)) for k in range(1, ROW)
    ]
    for copy in start_copies:
        copy.start()
    for copy in start_copies:
        copy.wait_recv()

    steps = as_float(y)
    for b in range(blocks):
        rows = slice(b * LANES, (b + 1) * LANES)
        incoming = decay(rates[b], steps) * start_ref[b] + row_start[b]
        across = jnp.transpose(incoming)
        same = iota((LANES, LANES), 1) // ORDER == iota((LANES, LANES), 0) // GROUP
        spread = jnp.where(same, jnp.concatenate([across] * (LANES // ORDER), axis=1), 0.0)
        carried = dot_split(split(spread), split(readout_ref[rows, :]), NN)
        gated_ref[rows, :] = (query_ref[rows, :] * (base_ref[rows, :] + carried)).astype(jnp.bfloat16)

    gated = gated_ref[...]
    part = out_ref.shape[0]
    half = part // 2

    def share(k, whose):
        owner = wrapped(x + k, RING) * 2 + whose
        rows = pl.ds(pl.multiple_of(owner * part, part), part)
        return jnp.dot(out_weight_ref[rows, :], gated, preferred_element_type=jnp.float32)

    pair_copies = [remote(given_ref.at[k], pair_ref.at[k], pair_sems.at[k], partner) for k in range(RING)]
    order = (2, 1, 3, 0)
    for k in order:
        given_ref[k] = share(k, 1 - core)
        pair_copies[k].start()
    for k in order:
        mine_ref[k] = share(k, core)

    top, bottom = pl.ds(0, half), pl.ds(half, half)
    relay_up = remote(mine_ref.at[2, top], relay_ref.at[0], ring_sems.at[0], at_ring(1))
    relay_down = remote(mine_ref.at[2, bottom], relay_ref.at[1], ring_sems.at[1], at_ring(-1))
    early_up = remote(mine_ref.at[1, bottom], last_ref.at[0, bottom], ring_sems.at[2], at_ring(1))
    early_down = remote(mine_ref.at[3, top], last_ref.at[1, top], ring_sems.at[3], at_ring(-1))
    late_up = remote(mine_ref.at[1, top], last_ref.at[0, top], ring_sems.at[4], at_ring(1))
    late_down = remote(mine_ref.at[3, bottom], last_ref.at[1, bottom], ring_sems.at[5], at_ring(-1))

    pair_copies[2].wait_recv()
    mine_ref[2] = mine_ref[2] + pair_ref[2]
    relay_up.start()
    relay_down.start()
    pair_copies[1].wait_recv()
    mine_ref[1] = mine_ref[1] + pair_ref[1]
    early_up.start()
    pair_copies[3].wait_recv()
    mine_ref[3] = mine_ref[3] + pair_ref[3]
    early_down.start()
    pair_copies[0].wait_recv()
    mine_ref[0] = mine_ref[0] + pair_ref[0]
    relay_up.wait_recv()
    mine_ref[1, top] = mine_ref[1, top] + relay_ref[0]
    late_up.start()
    relay_down.wait_recv()
    mine_ref[3, bottom] = mine_ref[3, bottom] + relay_ref[1]
    late_down.start()
    early_up.wait_recv()
    early_down.wait_recv()
    late_up.wait_recv()
    late_down.wait_recv()
    out_ref[...] = mine_ref[0] + last_ref[0] + last_ref[1]

    sent = halo_copies + [extra_copy] + row_copies + column_copies + start_copies + pair_copies
    sent += [relay_up, relay_down, early_up, early_down, late_up, late_down]
    for copy in sent:
        copy.wait_send()


def vmem():
    return pl.BlockSpec(memory_space=pltpu.VMEM)


def per_device(features, short_filter, medium_filter, rates, residues, skip_gain, out_weight):
    channels, length = features.shape[1:]
    groups = rates.shape[0]
    blocks = channels // LANES
    column = lax.axis_size("seq") // ROW
    part = out_weight.shape[0] // lax.axis_size("tp")
    f32 = jnp.float32
    weight = residues * jnp.sqrt(-jnp.expm1(-2.0 * rates))
    rate_blocks = jnp.repeat(rates.T, GROUP, axis=1).reshape(ORDER, blocks, LANES).transpose(1, 0, 2)
    tile = (ORDER, LANES)
    pairs = lambda n: pltpu.SemaphoreType.DMA((n, 2))
    return pl.pallas_call(
        layer_kernel,
        out_shape=jax.ShapeDtypeStruct((part, length), f32),
        in_specs=[vmem()] * 10,
        out_specs=vmem(),
        scratch_shapes=[
            pltpu.VMEM((3, channels, LANES), f32),
            pltpu.VMEM((3, 32, LANES), f32),
            pltpu.VMEM((3, 32, LANES), f32),
            pltpu.VMEM((3 * groups, length), f32),
            pltpu.VMEM((groups, length), f32),
            pltpu.VMEM((groups * ORDER, length), f32),
            pltpu.VMEM((groups * ORDER, length), f32),
            pltpu.VMEM((channels, length), f32),
            pltpu.VMEM((channels, length), f32),
            pltpu.VMEM((channels, length), f32),
            pltpu.VMEM((channels, length), jnp.bfloat16),
            pltpu.VMEM((blocks,) + tile, f32),
            pltpu.VMEM((ROW - 1, blocks) + tile, f32),
            pltpu.VMEM((blocks,) + tile, f32),
            pltpu.VMEM((column - 1,) + tile, f32),
            pltpu.VMEM((ROW,) + tile, f32),
            pltpu.VMEM((RING, part, length), f32),
            pltpu.VMEM((RING, part, length), f32),
            pltpu.VMEM((RING, part, length), f32),
            pltpu.VMEM((2, part // 2, length), f32),
            pltpu.VMEM((2, part, length), f32),
            pairs(4), pairs(ROW - 1), pairs(column - 1), pairs(ROW - 1), pairs(RING), pairs(6),
        ],
        compiler_params=pltpu.CompilerParams(
            collective_id=0, has_side_effects=True, vmem_limit_bytes=48 * 1024 * 1024
        ),
    )(
        features, short_filter.reshape(3 * groups, SHORT), medium_filter.reshape(3 * groups, MEDIUM),
        rates, weight, rates.reshape(-1, 1), weight.reshape(-1, 1), rate_blocks, skip_gain[:, None],
        out_weight,
    )


def solution(mesh):
    in_specs = (
        P(None, "tp", "seq"),
        P(None, "tp", None),
        P(None, "tp", None),
        P("tp", None),
        P("tp", None),
        P("tp"),
        P(None, "tp"),
    )
    out_specs = P("tp", "seq")
    return jax.shard_map(
        per_device, mesh=mesh, in_specs=in_specs, out_specs=out_specs, check_vma=False
    )
```

```python
import functools

import jax
import jax.numpy as jnp
from jax import lax
from jax.experimental import pallas as pl
from jax.experimental.pallas import tpu as pltpu
from jax.sharding import PartitionSpec as P

GROUP = 16
SHORT = 7
MEDIUM = 128
ORDER = 16
LANES = 128
ROW = 4
RING = 4
SUB = 8


def split(x):
    high = x.astype(jnp.bfloat16)
    return high, (x - high.astype(jnp.float32)).astype(jnp.bfloat16)


def dot_split(left, right, dims):
    a_high, a_low = left
    b_high, b_low = right
    one = functools.partial(
        lax.dot_general, dimension_numbers=(dims, ((), ())), preferred_element_type=jnp.float32
    )
    return one(a_high, b_high) + (one(a_high, b_low) + one(a_low, b_high))


NN = ((1,), (0,))
NT = ((1,), (1,))


def iota(shape, axis):
    return lax.broadcasted_iota(jnp.int32, shape, axis)


def upright(flat):
    rows, columns = flat.shape
    padded = jnp.concatenate([flat, jnp.zeros((rows, LANES - columns), jnp.float32)], axis=1)
    padded = jnp.concatenate([padded, jnp.zeros((LANES - rows, LANES), jnp.float32)], axis=0)
    return jnp.transpose(padded)[:columns]


def filter_tables(short_ref, medium_ref, taps_ref):
    branches, groups = medium_ref.shape[:2]
    for i in range(branches):
        medium, short = medium_ref[i], upright(short_ref[i])
        wide = jnp.concatenate([medium, jnp.zeros_like(medium)], axis=1)
        total = short[:, 0:1] * wide
        for j in range(1, SHORT):
            total = total + short[:, j : j + 1] * pltpu.roll(wide, j, 1)
        taps_ref[i * groups : (i + 1) * groups, :] = total


def modal_tables(rates_ref, weight_ref, rate_blocks_ref, kernel_ref, ending_ref, readout_ref):
    groups, length = kernel_ref.shape
    steps = iota((1, length), 1).astype(jnp.float32)
    all_rates, all_weight = upright(rates_ref[...]), upright(weight_ref[...])
    for b in range(groups // SUB):
        rates = all_rates[b * SUB : (b + 1) * SUB]
        weight = all_weight[b * SUB : (b + 1) * SUB]
        total = jnp.zeros((SUB, length), jnp.float32)
        for n in range(ORDER):
            rate, share = rates[:, n : n + 1], weight[:, n : n + 1]
            rows = slice((b * ORDER + n) * SUB, (b * ORDER + n + 1) * SUB)
            total = total + share * jnp.exp(-rate * steps)
            ending_ref[rows, :] = jnp.exp(-rate * (length - 1.0 - steps))
            readout_ref[rows, :] = share * jnp.exp(-rate * (steps + 1.0))
        kernel_ref[b * SUB : (b + 1) * SUB, :] = total
        wide = jnp.broadcast_to(rates[:, None, :], (SUB, GROUP, LANES)).reshape(SUB * GROUP, LANES)
        rate_blocks_ref[b] = jnp.transpose(wide)[:ORDER]


def toeplitz(row, rows):
    return pltpu.roll(jnp.broadcast_to(row, (rows, row.shape[1])), 0, 1, stride=1, stride_axis=0)


def filter_matrix(taps_row):
    rolled = toeplitz(taps_row, LANES)
    near, middle = rolled[:, :LANES], rolled[:, LANES:]
    causal = iota((LANES, LANES), 1) >= iota((LANES, LANES), 0)
    return split(jnp.concatenate(
        [jnp.where(causal, 0.0, near), middle, jnp.where(causal, near, 0.0)], axis=0
    ))


def filter_group(extra, halo, own, matrix):
    tiles = [extra, halo, own[:, :LANES], own[:, LANES:]]
    windows = jnp.concatenate(
        [jnp.concatenate(tiles[0:3], axis=1), jnp.concatenate(tiles[1:4], axis=1)], axis=0
    )
    result = dot_split(split(windows), matrix, NN)
    return jnp.concatenate([result[:GROUP], result[GROUP:]], axis=1)


def wrapped(index, count):
    return lax.rem(index + count, count)


def layer_kernel(
    features_hbm, short_ref, medium_ref, rates_ref, weight_ref, gain_ref, out_weight_hbm,
    out_ref,
    features_ref, out_weight_ref, rate_blocks_ref,
    matrix_high_ref, matrix_low_ref, long_high_ref, long_low_ref,
    halo_ref, packed_ref, extra_ref, taps_ref, kernel_ref, ending_ref, readout_ref,
    product_ref, query_ref, base_ref, gated_ref,
    state_ref, row_states_ref, total_ref, totals_ref, start_ref,
    given_ref, mine_ref, pair_ref, relay_ref, last_ref,
    near_sems, local_sems,
    halo_sems, row_sems, column_sems, start_sems, pair_sems, ring_sems,
):
    groups, length = kernel_ref.shape
    channels = product_ref.shape[0]
    blocks = channels // LANES
    count = lax.axis_size("seq")
    column = count // ROW
    seq, tp = lax.axis_index("seq"), lax.axis_index("tp")
    z, y = seq // ROW, lax.rem(seq, ROW)
    x, core = tp // 2, lax.rem(tp, 2)
    at_row = lambda k: (z * ROW + wrapped(y + k, ROW), tp)
    at_column = lambda k: (wrapped(z + k, column) * ROW + y, tp)
    at_ring = lambda k: (seq, wrapped(x + k, RING) * 2 + core)
    following, before = (wrapped(seq + 1, count), tp), (wrapped(seq - 1, count), tp)
    partner = (seq, x * 2 + 1 - core)

    def signal(semaphore, device):
        pl.semaphore_signal(semaphore, inc=1, device_id=device, device_id_type=pl.DeviceIdType.MESH)

    def remote(source, target, sems, device):
        return pltpu.make_async_remote_copy(
            src_ref=source, dst_ref=target, send_sem=sems.at[0], recv_sem=sems.at[1],
            device_id=device, device_id_type=pl.DeviceIdType.MESH,
        )

    barrier = pltpu.get_barrier_semaphore()
    peers = [following, before, partner, at_ring(1), at_ring(-1)]
    peers += [at_row(1), at_row(-1), at_column(1), at_column(-1)]
    for peer in peers:
        signal(barrier, peer)
    loads = [pltpu.make_async_copy(features_hbm.at[i], features_ref.at[i], local_sems.at[i]) for i in range(3)]
    loads.append(pltpu.make_async_copy(out_weight_hbm, out_weight_ref, local_sems.at[3]))
    for i in (1, 2, 0, 3):
        loads[i].start()
    halo_copies = [
        [
            remote(
                features_hbm.at[i, pl.ds(b * LANES, LANES), pl.ds(length - LANES, LANES)],
                halo_ref.at[i, pl.ds(b * LANES, LANES)], halo_sems.at[i * blocks + b], following,
            )
            for b in range(blocks)
        ]
        for i in range(3)
    ]
    extra_copy = remote(packed_ref, extra_ref, halo_sems.at[3 * blocks], following)
    lane = iota((32, LANES), 1) // 8
    for i in (1, 2, 0):
        loads[i].wait()
        packed = jnp.zeros((32, LANES), jnp.float32)
        for p in range(channels // 32):
            moved = pltpu.roll(features_ref[i, 32 * p : 32 * p + 32, 0:LANES], (8 * p + 8) % LANES, 1)
            packed = jnp.where(lane == p, moved, packed)
        packed_ref[i] = packed
    pl.semaphore_wait(barrier, len(peers))
    extra_copy.start()
    for b in range(blocks):
        halo_copies[1][b].start()
        halo_copies[2][b].start()
    for b in range(blocks):
        halo_copies[0][b].start()

    signal(near_sems.at[3], at_row(1))
    signal(near_sems.at[3], at_row(-1))
    signal(near_sems.at[0], at_column(1))
    signal(near_sems.at[0], at_column(-1))
    filter_tables(short_ref, medium_ref, taps_ref)
    pl.semaphore_wait(near_sems.at[3], 2)
    pl.semaphore_wait(near_sems.at[0], 2)
    signal(near_sems.at[1], at_column(2))
    signal(near_sems.at[1], at_column(-2))
    modal_tables(rates_ref, weight_ref, rate_blocks_ref, kernel_ref, ending_ref, readout_ref)
    pl.semaphore_wait(near_sems.at[1], 2)
    signal(near_sems.at[2], at_column(4))
    signal(near_sems.at[2], at_column(-4))
    inner = seq > 0

    def matrices_step(g, carry):
        for i in (1, 2):
            place = (i - 1) * groups + g
            high, low = filter_matrix(taps_ref[pl.ds(i * groups + g, 1), :])
            matrix_high_ref[place] = high
            matrix_low_ref[place] = low
        rolled = toeplitz(kernel_ref[pl.ds(g, 1), :], length)
        causal = iota((length, length), 1) >= iota((length, length), 0)
        high, low = split(jnp.where(causal, rolled, 0.0))
        long_high_ref[g] = high
        long_low_ref[g] = low
        return carry

    def branch(i, g, matrix):
        rows = pl.ds(pl.multiple_of(g * GROUP, GROUP), GROUP)
        packed = extra_ref[i, pl.ds(pl.multiple_of(lax.rem(g, 2) * GROUP, GROUP), GROUP), :]
        extra = pltpu.roll(packed, LANES - 8 - 8 * (g // 2), 1)
        zero = jnp.zeros((GROUP, LANES), jnp.float32)
        return filter_group(
            jnp.where(inner, extra, zero), jnp.where(inner, halo_ref[i, rows, :], zero),
            features_ref[i, rows, :], matrix,
        )

    def product_step(half, carry):
        for g in [half * 4 + u for u in range(4)]:
            rows = pl.ds(pl.multiple_of(g * GROUP, GROUP), GROUP)
            key = branch(1, g, (matrix_high_ref[g], matrix_low_ref[g]))
            value = branch(2, g, (matrix_high_ref[groups + g], matrix_low_ref[groups + g]))
            product = key * value
            product_ref[rows, :] = product
            base_ref[rows, :] = dot_split(split(product), (long_high_ref[g], long_low_ref[g]), NN)
        return carry

    def query_step(half, carry):
        for g in [half * 2 + u for u in range(2)]:
            rows = pl.ds(pl.multiple_of(g * GROUP, GROUP), GROUP)
            query_ref[rows, :] = branch(0, g, filter_matrix(taps_ref[pl.ds(g, 1), :]))
        return carry

    lax.fori_loop(0, groups, matrices_step, 0)
    pl.semaphore_wait(near_sems.at[2], 2)
    extra_copy.wait_recv()
    same = lax.rem(iota((LANES, LANES), 0), SUB) == iota((LANES, LANES), 1) // GROUP
    quarter_steps = groups // blocks // 4
    for b in range(blocks):
        halo_copies[1][b].wait_recv()
        halo_copies[2][b].wait_recv()
        lax.fori_loop(b * quarter_steps, (b + 1) * quarter_steps, product_step, 0)
        rows = slice(b * LANES, (b + 1) * LANES)
        full = dot_split(split(ending_ref[rows, :]), split(product_ref[rows, :]), NT)
        full = jnp.where(same, full, 0.0)
        state_ref[b] = jnp.sum(full.reshape(ORDER, SUB, LANES), axis=1)
    row_copies = [
        remote(state_ref, row_states_ref.at[k - 1], row_sems.at[k - 1], at_row(k)) for k in range(1, ROW)
    ]
    for copy in row_copies:
        copy.start()
    for b in range(blocks):
        rows = slice(b * LANES, (b + 1) * LANES)
        gain = jnp.transpose(jnp.broadcast_to(gain_ref[b : b + 1, :], (LANES, LANES)))
        base_ref[rows, :] = base_ref[rows, :] + jnp.concatenate([gain] * (length // LANES), axis=1) * product_ref[rows, :]

    for copy in halo_copies[0]:
        copy.wait_recv()
    lax.fori_loop(0, groups // 4, query_step, 0)

    for copy in row_copies:
        copy.wait_recv()
    rates = rate_blocks_ref[...]
    decay = lambda rates, steps: jnp.exp(-rates * (float(length) * steps))
    as_float = lambda value: lax.convert_element_type(value, jnp.float32)
    row_start = jnp.zeros(rates.shape, jnp.float32)
    row_total = decay(rates, as_float(ROW - 1 - y)) * state_ref[...]
    for k in range(1, ROW):
        state = row_states_ref[k - 1]
        row_start = row_start + jnp.where(k <= y, decay(rates, k - 1.0) * state, 0.0)
        row_total = row_total + decay(rates, as_float(ROW - 1 - wrapped(y - k, ROW))) * state
    total_ref[...] = row_total
    column_copies = [
        remote(total_ref.at[y], totals_ref.at[k - 1], column_sems.at[k - 1], at_column(k))
        for k in range(1, column)
    ]
    for copy in column_copies:
        copy.start()

    lax.fori_loop(groups // 4, groups // 2, query_step, 0)

    for copy in column_copies:
        copy.wait_recv()
    quarter = rate_blocks_ref[y]
    start = jnp.zeros(quarter.shape, jnp.float32)
    for k in range(1, column):
        start = start + jnp.where(k <= z, decay(quarter, float(ROW * (k - 1))) * totals_ref[k - 1], 0.0)
    start_ref[y] = start
    start_copies = [
        remote(start_ref.at[y], start_ref.at[y], start_sems.at[k - 1], at_row(k)) for k in range(1, ROW)
    ]
    for copy in start_copies:
        copy.start()
    for copy in start_copies:
        copy.wait_recv()

    steps = as_float(y)
    for b in range(blocks):
        rows = slice(b * LANES, (b + 1) * LANES)
        incoming = decay(rates[b], steps) * start_ref[b] + row_start[b]
        tall = jnp.broadcast_to(incoming[:, None, :], (ORDER, SUB, LANES)).reshape(LANES, LANES)
        spread = jnp.transpose(jnp.where(same, tall, 0.0))
        carried = dot_split(split(spread), split(readout_ref[rows, :]), NN)
        gated_ref[rows, :] = (query_ref[rows, :] * (base_ref[rows, :] + carried)).astype(jnp.bfloat16)

    loads[3].wait()
    gated = gated_ref[...]
    part = out_ref.shape[0]
    half = part // 2

    def share(k, whose):
        owner = wrapped(x + k, RING) * 2 + whose
        rows = pl.ds(pl.multiple_of(owner * part, part), part)
        return jnp.dot(out_weight_ref[rows, :], gated, preferred_element_type=jnp.float32)

    pair_copies = [remote(given_ref.at[k], pair_ref.at[k], pair_sems.at[k], partner) for k in range(RING)]
    order = (2, 1, 3, 0)
    for k in order:
        given_ref[k] = share(k, 1 - core)
        pair_copies[k].start()
    for k in order:
        mine_ref[k] = share(k, core)

    top, bottom = pl.ds(0, half), pl.ds(half, half)
    relay_up = remote(mine_ref.at[2, top], relay_ref.at[0], ring_sems.at[0], at_ring(1))
    relay_down = remote(mine_ref.at[2, bottom], relay_ref.at[1], ring_sems.at[1], at_ring(-1))
    early_up = remote(mine_ref.at[1, bottom], last_ref.at[0, bottom], ring_sems.at[2], at_ring(1))
    early_down = remote(mine_ref.at[3, top], last_ref.at[1, top], ring_sems.at[3], at_ring(-1))
    late_up = remote(mine_ref.at[1, top], last_ref.at[0, top], ring_sems.at[4], at_ring(1))
    late_down = remote(mine_ref.at[3, bottom], last_ref.at[1, bottom], ring_sems.at[5], at_ring(-1))

    pair_copies[2].wait_recv()
    mine_ref[2] = mine_ref[2] + pair_ref[2]
    relay_up.start()
    relay_down.start()
    pair_copies[1].wait_recv()
    mine_ref[1] = mine_ref[1] + pair_ref[1]
    early_up.start()
    pair_copies[3].wait_recv()
    mine_ref[3] = mine_ref[3] + pair_ref[3]
    early_down.start()
    pair_copies[0].wait_recv()
    mine_ref[0] = mine_ref[0] + pair_ref[0]
    relay_up.wait_recv()
    mine_ref[1, top] = mine_ref[1, top] + relay_ref[0]
    late_up.start()
    relay_down.wait_recv()
    mine_ref[3, bottom] = mine_ref[3, bottom] + relay_ref[1]
    late_down.start()
    early_up.wait_recv()
    early_down.wait_recv()
    late_up.wait_recv()
    late_down.wait_recv()
    out_ref[...] = mine_ref[0] + last_ref[0] + last_ref[1]

    sent = halo_copies[0] + halo_copies[1] + halo_copies[2] + [extra_copy] + row_copies + column_copies + start_copies + pair_copies
    sent += [relay_up, relay_down, early_up, early_down, late_up, late_down]
    for copy in sent:
        copy.wait_send()


def per_device(features, short_filter, medium_filter, rates, residues, skip_gain, out_weight):
    channels, length = features.shape[1:]
    groups = rates.shape[0]
    blocks = channels // LANES
    column = lax.axis_size("seq") // ROW
    part = out_weight.shape[0] // lax.axis_size("tp")
    f32 = jnp.float32
    weight = residues * jnp.sqrt(-jnp.expm1(-2.0 * rates))
    tile = (ORDER, LANES)
    half = jnp.bfloat16
    vmem = pl.BlockSpec(memory_space=pltpu.VMEM)
    hbm = pl.BlockSpec(memory_space=pltpu.HBM)
    pairs = lambda n: pltpu.SemaphoreType.DMA((n, 2))
    return pl.pallas_call(
        layer_kernel,
        out_shape=jax.ShapeDtypeStruct((part, length), f32),
        in_specs=[hbm] + [vmem] * 5 + [hbm],
        out_specs=vmem,
        scratch_shapes=[
            pltpu.VMEM(features.shape, f32),
            pltpu.VMEM(out_weight.shape, half),
            pltpu.VMEM((blocks,) + tile, f32),
            pltpu.VMEM((2 * groups, 3 * LANES, LANES), half),
            pltpu.VMEM((2 * groups, 3 * LANES, LANES), half),
            pltpu.VMEM((groups, length, length), half),
            pltpu.VMEM((groups, length, length), half),
            pltpu.VMEM((3, channels, LANES), f32),
            pltpu.VMEM((3, 32, LANES), f32),
            pltpu.VMEM((3, 32, LANES), f32),
            pltpu.VMEM((3 * groups, length), f32),
            pltpu.VMEM((groups, length), f32),
            pltpu.VMEM((groups * ORDER, length), f32),
            pltpu.VMEM((groups * ORDER, length), f32),
            pltpu.VMEM((channels, length), f32),
            pltpu.VMEM((channels, length), f32),
            pltpu.VMEM((channels, length), f32),
            pltpu.VMEM((channels, length), half),
            pltpu.VMEM((blocks,) + tile, f32),
            pltpu.VMEM((ROW - 1, blocks) + tile, f32),
            pltpu.VMEM((blocks,) + tile, f32),
            pltpu.VMEM((column - 1,) + tile, f32),
            pltpu.VMEM((ROW,) + tile, f32),
            pltpu.VMEM((RING, part, length), f32),
            pltpu.VMEM((RING, part, length), f32),
            pltpu.VMEM((RING, part, length), f32),
            pltpu.VMEM((2, part // 2, length), f32),
            pltpu.VMEM((2, part, length), f32),
            pltpu.SemaphoreType.REGULAR((4,)),
            pltpu.SemaphoreType.DMA((4,)),
            pairs(3 * blocks + 1), pairs(ROW - 1), pairs(column - 1), pairs(ROW - 1), pairs(RING), pairs(6),
        ],
        compiler_params=pltpu.CompilerParams(
            collective_id=0, has_side_effects=True, vmem_limit_bytes=58 * 1024 * 1024
        ),
    )(
        features, jnp.swapaxes(short_filter, 1, 2), medium_filter, rates.T, weight.T, skip_gain.reshape(blocks, LANES), out_weight,
    )


def solution(mesh):
    in_specs = (
        P(None, "tp", "seq"),
        P(None, "tp", None),
        P(None, "tp", None),
        P("tp", None),
        P("tp", None),
        P("tp"),
        P(None, "tp"),
    )
    out_specs = P("tp", "seq")
    return jax.shard_map(
        per_device, mesh=mesh, in_specs=in_specs, out_specs=out_specs, check_vma=False
    )
```

```python
import functools

import jax
import jax.numpy as jnp
from jax import lax
from jax.experimental import pallas as pl
from jax.experimental.pallas import tpu as pltpu
from jax.sharding import PartitionSpec as P

GROUP = 16
SHORT = 7
MEDIUM = 128
ORDER = 16
LANES = 128
ROW = 4
RING = 4
SUB = 8


def split(x):
    high = x.astype(jnp.bfloat16)
    return high, (x - high.astype(jnp.float32)).astype(jnp.bfloat16)


def dot_split(left, right, dims):
    a_high, a_low = left
    b_high, b_low = right
    one = functools.partial(
        lax.dot_general, dimension_numbers=(dims, ((), ())), preferred_element_type=jnp.float32
    )
    return one(a_high, b_high) + (one(a_high, b_low) + one(a_low, b_high))


NN = ((1,), (0,))
NT = ((1,), (1,))


def iota(shape, axis):
    return lax.broadcasted_iota(jnp.int32, shape, axis)


def upright(flat):
    rows, columns = flat.shape
    padded = jnp.concatenate([flat, jnp.zeros((rows, LANES - columns), jnp.float32)], axis=1)
    padded = jnp.concatenate([padded, jnp.zeros((LANES - rows, LANES), jnp.float32)], axis=0)
    return jnp.transpose(padded)[:columns]


def filter_tables(short_ref, medium_ref, taps_ref):
    branches, groups = medium_ref.shape[:2]
    for i in range(branches):
        medium, short = medium_ref[i], upright(short_ref[i])
        wide = jnp.concatenate([medium, jnp.zeros_like(medium)], axis=1)
        total = short[:, 0:1] * wide
        for j in range(1, SHORT):
            total = total + short[:, j : j + 1] * pltpu.roll(wide, j, 1)
        taps_ref[i * groups : (i + 1) * groups, :] = total


def one_less_decay(power):
    total = jnp.ones_like(power)
    for order in range(8, 1, -1):
        total = 1.0 - power * (1.0 / order) * total
    return power * total


def modal_tables(rates_ref, residues_ref, rate_blocks_ref, kernel_ref, ending_ref, readout_ref):
    groups, length = kernel_ref.shape
    steps = iota((1, length), 1).astype(jnp.float32)
    flat_rates = rates_ref[...]
    flat_weight = residues_ref[...] * jnp.sqrt(one_less_decay(2.0 * flat_rates))
    all_rates, all_weight = upright(flat_rates), upright(flat_weight)
    for b in range(groups // SUB):
        rates = all_rates[b * SUB : (b + 1) * SUB]
        weight = all_weight[b * SUB : (b + 1) * SUB]
        total = jnp.zeros((SUB, length), jnp.float32)
        for n in range(ORDER):
            rate, share = rates[:, n : n + 1], weight[:, n : n + 1]
            rows = slice((b * ORDER + n) * SUB, (b * ORDER + n + 1) * SUB)
            total = total + share * jnp.exp(-rate * steps)
            ending_ref[rows, :] = jnp.exp(-rate * (length - 1.0 - steps))
            readout_ref[rows, :] = share * jnp.exp(-rate * (steps + 1.0))
        kernel_ref[b * SUB : (b + 1) * SUB, :] = total
        wide = jnp.broadcast_to(rates[:, None, :], (SUB, GROUP, LANES)).reshape(SUB * GROUP, LANES)
        rate_blocks_ref[b] = jnp.transpose(wide)[:ORDER]


def toeplitz(row, rows):
    return pltpu.roll(jnp.broadcast_to(row, (rows, row.shape[1])), 0, 1, stride=1, stride_axis=0)


def filter_matrix(taps_row):
    rolled = toeplitz(taps_row, LANES)
    near, middle = rolled[:, :LANES], rolled[:, LANES:]
    causal = iota((LANES, LANES), 1) >= iota((LANES, LANES), 0)
    return split(jnp.concatenate(
        [jnp.where(causal, 0.0, near), middle, jnp.where(causal, near, 0.0)], axis=0
    ))


def long_matrix(row):
    rolled = toeplitz(row, LANES)
    near, middle = rolled[:, :LANES], rolled[:, LANES:]
    causal = iota((LANES, LANES), 1) >= iota((LANES, LANES), 0)
    return split(jnp.concatenate([middle, jnp.where(causal, near, 0.0)], axis=0))


def long_group(product, matrix):
    first, second = product[:, :LANES], product[:, LANES:]
    windows = jnp.concatenate(
        [jnp.concatenate([jnp.zeros_like(first), first], axis=1), product], axis=0
    )
    result = dot_split(split(windows), matrix, NN)
    return jnp.concatenate([result[:GROUP], result[GROUP:]], axis=1)


def filter_group(extra, halo, own, matrix):
    tiles = [extra, halo, own[:, :LANES], own[:, LANES:]]
    windows = jnp.concatenate(
        [jnp.concatenate(tiles[0:3], axis=1), jnp.concatenate(tiles[1:4], axis=1)], axis=0
    )
    result = dot_split(split(windows), matrix, NN)
    return jnp.concatenate([result[:GROUP], result[GROUP:]], axis=1)


def wrapped(index, count):
    return lax.rem(index + count, count)


def layer_kernel(
    features_hbm, short_hbm, medium_hbm, rates_hbm, residues_hbm, gain_hbm, out_weight_hbm,
    out_ref,
    features_ref, short_ref, medium_ref, rates_ref, residues_ref, gain_ref, out_weight_ref, rate_blocks_ref,
    matrix_high_ref, matrix_low_ref, long_high_ref, long_low_ref,
    halo_ref, packed_ref, extra_ref, taps_ref, kernel_ref, ending_ref, readout_ref,
    product_ref, query_ref, base_ref, gated_ref,
    state_ref, row_states_ref, total_ref, totals_ref, start_ref,
    given_ref, mine_ref, pair_ref, relay_ref, last_ref,
    near_sems, local_sems,
    halo_sems, row_sems, column_sems, start_sems, pair_sems, ring_sems,
):
    groups, length = kernel_ref.shape
    channels = product_ref.shape[0]
    blocks = channels // LANES
    count = lax.axis_size("seq")
    column = count // ROW
    seq, tp = lax.axis_index("seq"), lax.axis_index("tp")
    z, y = seq // ROW, lax.rem(seq, ROW)
    x, core = tp // 2, lax.rem(tp, 2)
    at_row = lambda k: (z * ROW + wrapped(y + k, ROW), tp)
    at_column = lambda k: (wrapped(z + k, column) * ROW + y, tp)
    at_ring = lambda k: (seq, wrapped(x + k, RING) * 2 + core)
    following, before = (wrapped(seq + 1, count), tp), (wrapped(seq - 1, count), tp)
    partner = (seq, x * 2 + 1 - core)

    def signal(semaphore, device):
        pl.semaphore_signal(semaphore, inc=1, device_id=device, device_id_type=pl.DeviceIdType.MESH)

    def remote(source, target, sems, device):
        return pltpu.make_async_remote_copy(
            src_ref=source, dst_ref=target, send_sem=sems.at[0], recv_sem=sems.at[1],
            device_id=device, device_id_type=pl.DeviceIdType.MESH,
        )

    barrier = pltpu.get_barrier_semaphore()
    peers = [following, before, partner, at_ring(1), at_ring(-1)]
    peers += [at_row(1), at_row(-1), at_column(1), at_column(-1)]
    for peer in peers:
        signal(barrier, peer)
    whole = [short_hbm, medium_hbm, rates_hbm, residues_hbm, gain_hbm, out_weight_hbm]
    kept = [short_ref, medium_ref, rates_ref, residues_ref, gain_ref, out_weight_ref]
    loads = [pltpu.make_async_copy(features_hbm.at[i], features_ref.at[i], local_sems.at[i]) for i in range(3)]
    loads += [pltpu.make_async_copy(a, b, local_sems.at[3 + k]) for k, (a, b) in enumerate(zip(whole, kept))]
    for i in (1, 2, 0, 3, 4, 5, 6, 7, 8):
        loads[i].start()
    halo_copies = [
        [
            remote(
                features_hbm.at[i, pl.ds(b * LANES, LANES), pl.ds(length - LANES, LANES)],
                halo_ref.at[i, pl.ds(b * LANES, LANES)], halo_sems.at[i * blocks + b], following,
            )
            for b in range(blocks)
        ]
        for i in range(3)
    ]
    extra_copy = remote(packed_ref, extra_ref, halo_sems.at[3 * blocks], following)
    lane = iota((32, LANES), 1) // 8
    pl.semaphore_wait(barrier, len(peers))
    halo_copies[1][0].start()
    halo_copies[2][0].start()
    for i in (1, 2, 0):
        loads[i].wait()
        packed = jnp.zeros((32, LANES), jnp.float32)
        for p in range(channels // 32):
            moved = pltpu.roll(features_ref[i, 32 * p : 32 * p + 32, 0:LANES], (8 * p + 8) % LANES, 1)
            packed = jnp.where(lane == p, moved, packed)
        packed_ref[i] = packed
    extra_copy.start()
    for b in range(1, blocks):
        halo_copies[1][b].start()
        halo_copies[2][b].start()
    for b in range(blocks):
        halo_copies[0][b].start()

    signal(near_sems.at[3], at_row(1))
    signal(near_sems.at[3], at_row(-1))
    signal(near_sems.at[0], at_column(1))
    signal(near_sems.at[0], at_column(-1))
    for i in range(3, 8):
        loads[i].wait()
    filter_tables(short_ref, medium_ref, taps_ref)
    pl.semaphore_wait(near_sems.at[3], 2)
    pl.semaphore_wait(near_sems.at[0], 2)
    signal(near_sems.at[1], at_column(2))
    signal(near_sems.at[1], at_column(-2))
    modal_tables(rates_ref, residues_ref, rate_blocks_ref, kernel_ref, ending_ref, readout_ref)
    pl.semaphore_wait(near_sems.at[1], 2)
    signal(near_sems.at[2], at_column(4))
    signal(near_sems.at[2], at_column(-4))
    inner = seq > 0

    def matrices_step(half, carry):
        for g in [half * 2 + u for u in range(2)]:
            for i in (1, 2):
                place = (i - 1) * groups + g
                high, low = filter_matrix(taps_ref[pl.ds(i * groups + g, 1), :])
                matrix_high_ref[place] = high
                matrix_low_ref[place] = low
            high, low = long_matrix(kernel_ref[pl.ds(g, 1), :])
            long_high_ref[g] = high
            long_low_ref[g] = low
        return carry

    def branch(i, g, matrix):
        rows = pl.ds(pl.multiple_of(g * GROUP, GROUP), GROUP)
        packed = extra_ref[i, pl.ds(pl.multiple_of(lax.rem(g, 2) * GROUP, GROUP), GROUP), :]
        extra = pltpu.roll(packed, LANES - 8 - 8 * (g // 2), 1)
        zero = jnp.zeros((GROUP, LANES), jnp.float32)
        return filter_group(
            jnp.where(inner, extra, zero), jnp.where(inner, halo_ref[i, rows, :], zero),
            features_ref[i, rows, :], matrix,
        )

    def product_step(half, carry):
        for g in [half * 4 + u for u in range(4)]:
            rows = pl.ds(pl.multiple_of(g * GROUP, GROUP), GROUP)
            key = branch(1, g, (matrix_high_ref[g], matrix_low_ref[g]))
            value = branch(2, g, (matrix_high_ref[groups + g], matrix_low_ref[groups + g]))
            product = key * value
            product_ref[rows, :] = product
            base_ref[rows, :] = long_group(product, (long_high_ref[g], long_low_ref[g]))
        return carry

    def query_step(half, carry):
        for g in [half * 2 + u for u in range(2)]:
            rows = pl.ds(pl.multiple_of(g * GROUP, GROUP), GROUP)
            query_ref[rows, :] = branch(0, g, filter_matrix(taps_ref[pl.ds(g, 1), :]))
        return carry

    lax.fori_loop(0, groups // 2, matrices_step, 0)
    pl.semaphore_wait(near_sems.at[2], 2)
    extra_copy.wait_recv()
    same = lax.rem(iota((LANES, LANES), 0), SUB) == iota((LANES, LANES), 1) // GROUP
    quarter_steps = groups // blocks // 4
    for b in range(blocks):
        halo_copies[1][b].wait_recv()
        halo_copies[2][b].wait_recv()
        lax.fori_loop(b * quarter_steps, (b + 1) * quarter_steps, product_step, 0)
        rows = slice(b * LANES, (b + 1) * LANES)
        full = dot_split(split(ending_ref[rows, :]), split(product_ref[rows, :]), NT)
        full = jnp.where(same, full, 0.0)
        state_ref[b] = jnp.sum(full.reshape(ORDER, SUB, LANES), axis=1)
    row_copies = [
        remote(state_ref, row_states_ref.at[k - 1], row_sems.at[k - 1], at_row(k)) for k in range(1, ROW)
    ]
    for copy in row_copies:
        copy.start()
    for b in range(blocks):
        rows = slice(b * LANES, (b + 1) * LANES)
        gain = jnp.transpose(jnp.broadcast_to(gain_ref[b : b + 1, :], (LANES, LANES)))
        base_ref[rows, :] = base_ref[rows, :] + jnp.concatenate([gain] * (length // LANES), axis=1) * product_ref[rows, :]

    rates = rate_blocks_ref[...]
    decay = lambda rates, steps: jnp.exp(-rates * (float(length) * steps))
    as_float = lambda value: lax.convert_element_type(value, jnp.float32)
    to_total = [decay(rates, as_float(ROW - 1 - wrapped(y - k, ROW))) for k in range(ROW)]
    to_start = [jnp.where(k <= y, decay(rates, k - 1.0), 0.0) for k in range(1, ROW)]
    row_start = jnp.zeros(rates.shape, jnp.float32)
    row_total = to_total[0] * state_ref[...]
    for k in range(1, ROW):
        row_copies[k - 1].wait_recv()
        state = row_states_ref[k - 1]
        row_start = row_start + to_start[k - 1] * state
        row_total = row_total + to_total[k] * state
    total_ref[...] = row_total
    column_copies = [
        remote(total_ref.at[y], totals_ref.at[k - 1], column_sems.at[k - 1], at_column(k))
        for k in range(1, column)
    ]
    for copy in column_copies:
        copy.start()

    for copy in halo_copies[0]:
        copy.wait_recv()
    lax.fori_loop(0, groups // 2, query_step, 0)

    quarter = rate_blocks_ref[y]
    to_here = [
        jnp.where(k <= z, decay(quarter, float(ROW * (k - 1))), 0.0) for k in range(1, column)
    ]
    through_row = decay(rates, as_float(y))
    start = jnp.zeros(quarter.shape, jnp.float32)
    for k in range(1, column):
        column_copies[k - 1].wait_recv()
        start = start + to_here[k - 1] * totals_ref[k - 1]
    start_ref[y] = start
    start_copies = [
        remote(start_ref.at[y], start_ref.at[y], start_sems.at[k - 1], at_row(k)) for k in range(1, ROW)
    ]
    for copy in start_copies:
        copy.start()
    for copy in start_copies:
        copy.wait_recv()

    for b in range(blocks):
        rows = slice(b * LANES, (b + 1) * LANES)
        incoming = through_row[b] * start_ref[b] + row_start[b]
        tall = jnp.broadcast_to(incoming[:, None, :], (ORDER, SUB, LANES)).reshape(LANES, LANES)
        spread = jnp.transpose(jnp.where(same, tall, 0.0))
        carried = dot_split(split(spread), split(readout_ref[rows, :]), NN)
        gated_ref[rows, :] = (query_ref[rows, :] * (base_ref[rows, :] + carried)).astype(jnp.bfloat16)

    loads[8].wait()
    gated = gated_ref[...]
    part = out_ref.shape[0]
    half = part // 2

    def share(k, whose):
        owner = wrapped(x + k, RING) * 2 + whose
        rows = pl.ds(pl.multiple_of(owner * part, part), part)
        return jnp.dot(out_weight_ref[rows, :], gated, preferred_element_type=jnp.float32)

    pair_copies = [remote(given_ref.at[k], pair_ref.at[k], pair_sems.at[k], partner) for k in range(RING)]
    top, bottom = pl.ds(0, half), pl.ds(half, half)
    relay_up = remote(mine_ref.at[2, top], relay_ref.at[0], ring_sems.at[0], at_ring(1))
    relay_down = remote(mine_ref.at[2, bottom], relay_ref.at[1], ring_sems.at[1], at_ring(-1))
    early_up = remote(mine_ref.at[1, bottom], last_ref.at[0, bottom], ring_sems.at[2], at_ring(1))
    early_down = remote(mine_ref.at[3, top], last_ref.at[1, top], ring_sems.at[3], at_ring(-1))
    late_up = remote(mine_ref.at[1, top], last_ref.at[0, top], ring_sems.at[4], at_ring(1))
    late_down = remote(mine_ref.at[3, bottom], last_ref.at[1, bottom], ring_sems.at[5], at_ring(-1))

    def offer(k):
        given_ref[k] = share(k, 1 - core)
        pair_copies[k].start()

    def meet(k):
        pair_copies[k].wait_recv()
        mine_ref[k] = mine_ref[k] + pair_ref[k]

    offer(2)
    offer(1)
    mine_ref[2] = share(2, core)
    offer(3)
    meet(2)
    relay_up.start()
    relay_down.start()
    mine_ref[1] = share(1, core)
    meet(1)
    early_up.start()
    mine_ref[3] = share(3, core)
    meet(3)
    early_down.start()
    offer(0)
    mine_ref[0] = share(0, core)
    meet(0)
    relay_up.wait_recv()
    mine_ref[1, top] = mine_ref[1, top] + relay_ref[0]
    late_up.start()
    relay_down.wait_recv()
    mine_ref[3, bottom] = mine_ref[3, bottom] + relay_ref[1]
    late_down.start()
    early_up.wait_recv()
    early_down.wait_recv()
    late_up.wait_recv()
    late_down.wait_recv()
    out_ref[...] = mine_ref[0] + last_ref[0] + last_ref[1]

    sent = halo_copies[0] + halo_copies[1] + halo_copies[2] + [extra_copy] + row_copies + column_copies + start_copies + pair_copies
    sent += [relay_up, relay_down, early_up, early_down, late_up, late_down]
    for copy in sent:
        copy.wait_send()


def per_device(features, short_filter, medium_filter, rates, residues, skip_gain, out_weight):
    channels, length = features.shape[1:]
    groups = rates.shape[0]
    blocks = channels // LANES
    column = lax.axis_size("seq") // ROW
    part = out_weight.shape[0] // lax.axis_size("tp")
    f32 = jnp.float32
    tile = (ORDER, LANES)
    half = jnp.bfloat16
    vmem = pl.BlockSpec(memory_space=pltpu.VMEM)
    hbm = pl.BlockSpec(memory_space=pltpu.HBM)
    pairs = lambda n: pltpu.SemaphoreType.DMA((n, 2))
    return pl.pallas_call(
        layer_kernel,
        out_shape=pltpu.VMEM((part, length), f32),
        in_specs=[hbm] * 7,
        out_specs=vmem,
        scratch_shapes=[
            pltpu.VMEM(features.shape, f32),
            pltpu.VMEM((3, SHORT, groups), f32),
            pltpu.VMEM(medium_filter.shape, f32),
            pltpu.VMEM((ORDER, groups), f32),
            pltpu.VMEM((ORDER, groups), f32),
            pltpu.VMEM((blocks, LANES), f32),
            pltpu.VMEM(out_weight.shape, half),
            pltpu.VMEM((blocks,) + tile, f32),
            pltpu.VMEM((2 * groups, 3 * LANES, LANES), half),
            pltpu.VMEM((2 * groups, 3 * LANES, LANES), half),
            pltpu.VMEM((groups, 2 * LANES, LANES), half),
            pltpu.VMEM((groups, 2 * LANES, LANES), half),
            pltpu.VMEM((3, channels, LANES), f32),
            pltpu.VMEM((3, 32, LANES), f32),
            pltpu.VMEM((3, 32, LANES), f32),
            pltpu.VMEM((3 * groups, length), f32),
            pltpu.VMEM((groups, length), f32),
            pltpu.VMEM((groups * ORDER, length), f32),
            pltpu.VMEM((groups * ORDER, length), f32),
            pltpu.VMEM((channels, length), f32),
            pltpu.VMEM((channels, length), f32),
            pltpu.VMEM((channels, length), f32),
            pltpu.VMEM((channels, length), half),
            pltpu.VMEM((blocks,) + tile, f32),
            pltpu.VMEM((ROW - 1, blocks) + tile, f32),
            pltpu.VMEM((blocks,) + tile, f32),
            pltpu.VMEM((column - 1,) + tile, f32),
            pltpu.VMEM((ROW,) + tile, f32),
            pltpu.VMEM((RING, part, length), f32),
            pltpu.VMEM((RING, part, length), f32),
            pltpu.VMEM((RING, part, length), f32),
            pltpu.VMEM((2, part // 2, length), f32),
            pltpu.VMEM((2, part, length), f32),
            pltpu.SemaphoreType.REGULAR((4,)),
            pltpu.SemaphoreType.DMA((9,)),
            pairs(3 * blocks + 1), pairs(ROW - 1), pairs(column - 1), pairs(ROW - 1), pairs(RING), pairs(6),
        ],
        compiler_params=pltpu.CompilerParams(
            collective_id=0, has_side_effects=True, vmem_limit_bytes=58 * 1024 * 1024
        ),
    )(
        features, jnp.swapaxes(short_filter, 1, 2), medium_filter, rates.T, residues.T, skip_gain.reshape(blocks, LANES), out_weight,
    )


def solution(mesh):
    in_specs = (
        P(None, "tp", "seq"),
        P(None, "tp", None),
        P(None, "tp", None),
        P("tp", None),
        P("tp", None),
        P("tp"),
        P(None, "tp"),
    )
    out_specs = P("tp", "seq")
    return jax.shard_map(
        per_device, mesh=mesh, in_specs=in_specs, out_specs=out_specs, check_vma=False
    )
```

```python
import functools

import jax
import jax.numpy as jnp
from jax import lax
from jax.experimental import pallas as pl
from jax.experimental.pallas import tpu as pltpu
from jax.sharding import PartitionSpec as P

GROUP = 16
SHORT = 7
MEDIUM = 128
ORDER = 16
LANES = 128
ROW = 4
RING = 4
PARTS = 8
SUB = 8


def split(x):
    high = x.astype(jnp.bfloat16)
    return high, (x - high.astype(jnp.float32)).astype(jnp.bfloat16)


def dot_split(left, right, dims):
    a_high, a_low = left
    b_high, b_low = right
    one = functools.partial(
        lax.dot_general, dimension_numbers=(dims, ((), ())), preferred_element_type=jnp.float32
    )
    return one(a_high, b_high) + (one(a_high, b_low) + one(a_low, b_high))


NN = ((1,), (0,))
NT = ((1,), (1,))


def iota(shape, axis):
    return lax.broadcasted_iota(jnp.int32, shape, axis)


def upright(flat):
    rows, columns = flat.shape
    padded = jnp.concatenate([flat, jnp.zeros((rows, LANES - columns), jnp.float32)], axis=1)
    padded = jnp.concatenate([padded, jnp.zeros((LANES - rows, LANES), jnp.float32)], axis=0)
    return jnp.transpose(padded)[:columns]


def filter_tables(short_ref, medium_ref, taps_ref):
    branches, groups = medium_ref.shape[:2]
    for i in range(branches):
        medium, short = medium_ref[i], upright(short_ref[i])
        wide = jnp.concatenate([medium, jnp.zeros_like(medium)], axis=1)
        total = short[:, 0:1] * wide
        for j in range(1, SHORT):
            total = total + short[:, j : j + 1] * pltpu.roll(wide, j, 1)
        taps_ref[i * groups : (i + 1) * groups, :] = total


def one_less_decay(power):
    total = jnp.ones_like(power)
    for order in range(8, 1, -1):
        total = 1.0 - power * (1.0 / order) * total
    return power * total


def modal_tables(rates_ref, residues_ref, rate_blocks_ref, kernel_ref, ending_ref, readout_ref):
    groups, length = kernel_ref.shape
    steps = iota((1, length), 1).astype(jnp.float32)
    flat_rates = rates_ref[...]
    flat_weight = residues_ref[...] * jnp.sqrt(one_less_decay(2.0 * flat_rates))
    all_rates, all_weight = upright(flat_rates), upright(flat_weight)
    for b in range(groups // SUB):
        rates = all_rates[b * SUB : (b + 1) * SUB]
        weight = all_weight[b * SUB : (b + 1) * SUB]
        total = jnp.zeros((SUB, length), jnp.float32)
        for n in range(ORDER):
            rate, share = rates[:, n : n + 1], weight[:, n : n + 1]
            rows = slice((b * ORDER + n) * SUB, (b * ORDER + n + 1) * SUB)
            total = total + share * jnp.exp(-rate * steps)
            ending_ref[rows, :] = jnp.exp(-rate * (length - 1.0 - steps))
            readout_ref[rows, :] = share * jnp.exp(-rate * (steps + 1.0))
        kernel_ref[b * SUB : (b + 1) * SUB, :] = total
        wide = jnp.broadcast_to(rates[:, None, :], (SUB, GROUP, LANES)).reshape(SUB * GROUP, LANES)
        rate_blocks_ref[b] = jnp.transpose(wide)[:ORDER]


def toeplitz(row, rows):
    return pltpu.roll(jnp.broadcast_to(row, (rows, row.shape[1])), 0, 1, stride=1, stride_axis=0)


def filter_matrix(taps_row):
    rolled = toeplitz(taps_row, LANES)
    near, middle = rolled[:, :LANES], rolled[:, LANES:]
    causal = iota((LANES, LANES), 1) >= iota((LANES, LANES), 0)
    return split(jnp.concatenate(
        [jnp.where(causal, 0.0, near), middle, jnp.where(causal, near, 0.0)], axis=0
    ))


def long_matrix(row):
    rolled = toeplitz(row, LANES)
    near, middle = rolled[:, :LANES], rolled[:, LANES:]
    causal = iota((LANES, LANES), 1) >= iota((LANES, LANES), 0)
    return split(jnp.concatenate([middle, jnp.where(causal, near, 0.0)], axis=0))


def long_group(product, matrix):
    first, second = product[:, :LANES], product[:, LANES:]
    windows = jnp.concatenate(
        [jnp.concatenate([jnp.zeros_like(first), first], axis=1), product], axis=0
    )
    result = dot_split(split(windows), matrix, NN)
    return jnp.concatenate([result[:GROUP], result[GROUP:]], axis=1)


def filter_group(extra, halo, own, matrix):
    tiles = [extra, halo, own[:, :LANES], own[:, LANES:]]
    windows = jnp.concatenate(
        [jnp.concatenate(tiles[0:3], axis=1), jnp.concatenate(tiles[1:4], axis=1)], axis=0
    )
    result = dot_split(split(windows), matrix, NN)
    return jnp.concatenate([result[:GROUP], result[GROUP:]], axis=1)


def wrapped(index, count):
    return lax.rem(index + count, count)


def farthest_first(count):
    return sorted(range(1, count), key=lambda k: -min(k, count - k))


def layer_kernel(
    features_hbm, short_hbm, medium_hbm, rates_hbm, residues_hbm, gain_hbm, out_weight_hbm,
    out_ref,
    features_ref, short_ref, medium_ref, rates_ref, residues_ref, gain_ref, out_weight_ref, rate_blocks_ref,
    matrix_high_ref, matrix_low_ref, long_high_ref, long_low_ref,
    halo_ref, packed_ref, extra_ref, taps_ref, kernel_ref, ending_ref, readout_ref,
    product_ref, query_ref, base_ref, gated_ref,
    state_ref, row_states_ref, total_ref, totals_ref, start_ref,
    given_ref, mine_ref, pair_ref, relay_ref, last_ref,
    near_sems, local_sems,
    halo_sems, row_sems, column_sems, start_sems, pair_sems, ring_sems,
):
    groups, length = kernel_ref.shape
    channels = product_ref.shape[0]
    blocks = channels // LANES
    count = lax.axis_size("seq")
    column = count // ROW
    seq, tp = lax.axis_index("seq"), lax.axis_index("tp")
    z, y = seq // ROW, lax.rem(seq, ROW)
    x, core = tp // 2, lax.rem(tp, 2)
    at_row = lambda k: (z * ROW + wrapped(y + k, ROW), tp)
    at_column = lambda k: (wrapped(z + k, column) * ROW + y, tp)
    at_ring = lambda k: (seq, wrapped(x + k, RING) * 2 + core)
    following, before = (wrapped(seq + 1, count), tp), (wrapped(seq - 1, count), tp)
    partner = (seq, x * 2 + 1 - core)

    def signal(semaphore, device):
        pl.semaphore_signal(semaphore, inc=1, device_id=device, device_id_type=pl.DeviceIdType.MESH)

    def remote(source, target, sems, device):
        return pltpu.make_async_remote_copy(
            src_ref=source, dst_ref=target, send_sem=sems.at[0], recv_sem=sems.at[1],
            device_id=device, device_id_type=pl.DeviceIdType.MESH,
        )

    barrier = pltpu.get_barrier_semaphore()
    peers = [following, before, partner, at_ring(1), at_ring(-1)]
    peers += [at_row(1), at_row(-1), at_column(1), at_column(-1)]
    for peer in peers:
        signal(barrier, peer)
    whole = [short_hbm, medium_hbm, rates_hbm, residues_hbm, gain_hbm, out_weight_hbm]
    kept = [short_ref, medium_ref, rates_ref, residues_ref, gain_ref, out_weight_ref]
    loads = [pltpu.make_async_copy(features_hbm.at[i], features_ref.at[i], local_sems.at[i]) for i in range(3)]
    loads += [pltpu.make_async_copy(a, b, local_sems.at[3 + k]) for k, (a, b) in enumerate(zip(whole, kept))]
    for i in (1, 2, 0, 3, 4, 5, 6, 7, 8):
        loads[i].start()
    depth = channels // PARTS
    halo_copies = [
        [
            remote(
                features_hbm.at[i, pl.ds(b * depth, depth), pl.ds(length - LANES, LANES)],
                halo_ref.at[i, pl.ds(b * depth, depth)], halo_sems.at[i * PARTS + b], following,
            )
            for b in range(PARTS)
        ]
        for i in range(3)
    ]
    extra_copy = remote(packed_ref, extra_ref, halo_sems.at[3 * PARTS], following)
    lane = iota((32, LANES), 1) // 8
    pl.semaphore_wait(barrier, len(peers))
    for b in range(2):
        halo_copies[1][b].start()
        halo_copies[2][b].start()
    for i in (1, 2, 0):
        loads[i].wait()
        packed = jnp.zeros((32, LANES), jnp.float32)
        for p in range(channels // 32):
            moved = pltpu.roll(features_ref[i, 32 * p : 32 * p + 32, 0:LANES], (8 * p + 8) % LANES, 1)
            packed = jnp.where(lane == p, moved, packed)
        packed_ref[i] = packed
    extra_copy.start()
    for b in range(2, PARTS):
        halo_copies[1][b].start()
        halo_copies[2][b].start()
    for b in range(PARTS):
        halo_copies[0][b].start()

    signal(near_sems.at[3], at_row(1))
    signal(near_sems.at[3], at_row(-1))
    signal(near_sems.at[0], at_column(1))
    signal(near_sems.at[0], at_column(-1))
    for i in range(3, 8):
        loads[i].wait()
    filter_tables(short_ref, medium_ref, taps_ref)
    pl.semaphore_wait(near_sems.at[3], 2)
    pl.semaphore_wait(near_sems.at[0], 2)
    signal(near_sems.at[1], at_column(2))
    signal(near_sems.at[1], at_column(-2))
    modal_tables(rates_ref, residues_ref, rate_blocks_ref, kernel_ref, ending_ref, readout_ref)
    pl.semaphore_wait(near_sems.at[1], 2)
    signal(near_sems.at[2], at_column(4))
    signal(near_sems.at[2], at_column(-4))
    inner = seq > 0

    def matrices_step(half, carry):
        for g in [half * 2 + u for u in range(2)]:
            for i in (1, 2):
                place = (i - 1) * groups + g
                high, low = filter_matrix(taps_ref[pl.ds(i * groups + g, 1), :])
                matrix_high_ref[place] = high
                matrix_low_ref[place] = low
            high, low = long_matrix(kernel_ref[pl.ds(g, 1), :])
            long_high_ref[g] = high
            long_low_ref[g] = low
        return carry

    def branch(i, g, matrix):
        rows = pl.ds(pl.multiple_of(g * GROUP, GROUP), GROUP)
        packed = extra_ref[i, pl.ds(pl.multiple_of(lax.rem(g, 2) * GROUP, GROUP), GROUP), :]
        extra = pltpu.roll(packed, LANES - 8 - 8 * (g // 2), 1)
        zero = jnp.zeros((GROUP, LANES), jnp.float32)
        return filter_group(
            jnp.where(inner, extra, zero), jnp.where(inner, halo_ref[i, rows, :], zero),
            features_ref[i, rows, :], matrix,
        )

    def product_step(half, carry):
        for g in [half * 4 + u for u in range(4)]:
            rows = pl.ds(pl.multiple_of(g * GROUP, GROUP), GROUP)
            key = branch(1, g, (matrix_high_ref[g], matrix_low_ref[g]))
            value = branch(2, g, (matrix_high_ref[groups + g], matrix_low_ref[groups + g]))
            product = key * value
            product_ref[rows, :] = product
            base_ref[rows, :] = long_group(product, (long_high_ref[g], long_low_ref[g]))
        return carry

    def query_step(half, carry):
        for g in [half * 2 + u for u in range(2)]:
            rows = pl.ds(pl.multiple_of(g * GROUP, GROUP), GROUP)
            query_ref[rows, :] = branch(0, g, filter_matrix(taps_ref[pl.ds(g, 1), :]))
        return carry

    lax.fori_loop(0, groups // 2, matrices_step, 0)
    pl.semaphore_wait(near_sems.at[2], 2)
    extra_copy.wait_recv()
    same = lax.rem(iota((LANES, LANES), 0), SUB) == iota((LANES, LANES), 1) // GROUP
    part_steps = groups // PARTS // 4
    for b in range(blocks):
        for p in range(b * PARTS // blocks, (b + 1) * PARTS // blocks):
            halo_copies[1][p].wait_recv()
            halo_copies[2][p].wait_recv()
            lax.fori_loop(p * part_steps, (p + 1) * part_steps, product_step, 0)
        rows = slice(b * LANES, (b + 1) * LANES)
        full = dot_split(split(ending_ref[rows, :]), split(product_ref[rows, :]), NT)
        full = jnp.where(same, full, 0.0)
        state_ref[b] = jnp.sum(full.reshape(ORDER, SUB, LANES), axis=1)
    row_copies = [
        remote(state_ref, row_states_ref.at[k - 1], row_sems.at[k - 1], at_row(k)) for k in range(1, ROW)
    ]
    for k in farthest_first(ROW):
        row_copies[k - 1].start()
    for b in range(blocks):
        rows = slice(b * LANES, (b + 1) * LANES)
        gain = jnp.transpose(jnp.broadcast_to(gain_ref[b : b + 1, :], (LANES, LANES)))
        base_ref[rows, :] = base_ref[rows, :] + jnp.concatenate([gain] * (length // LANES), axis=1) * product_ref[rows, :]

    rates = rate_blocks_ref[...]
    decay = lambda rates, steps: jnp.exp(-rates * (float(length) * steps))
    as_float = lambda value: lax.convert_element_type(value, jnp.float32)
    to_total = [decay(rates, as_float(ROW - 1 - wrapped(y - k, ROW))) for k in range(ROW)]
    to_start = [jnp.where(k <= y, decay(rates, k - 1.0), 0.0) for k in range(1, ROW)]
    row_start = jnp.zeros(rates.shape, jnp.float32)
    row_total = to_total[0] * state_ref[...]
    for k in range(1, ROW):
        row_copies[k - 1].wait_recv()
        state = row_states_ref[k - 1]
        row_start = row_start + to_start[k - 1] * state
        row_total = row_total + to_total[k] * state
    total_ref[...] = row_total
    column_copies = [
        remote(total_ref.at[y], totals_ref.at[k - 1], column_sems.at[k - 1], at_column(k))
        for k in range(1, column)
    ]
    for k in farthest_first(column):
        column_copies[k - 1].start()

    for copy in halo_copies[0]:
        copy.wait_recv()
    lax.fori_loop(0, groups // 2, query_step, 0)

    quarter = rate_blocks_ref[y]
    to_here = [
        jnp.where(k <= z, decay(quarter, float(ROW * (k - 1))), 0.0) for k in range(1, column)
    ]
    through_row = decay(rates, as_float(y))
    start = jnp.zeros(quarter.shape, jnp.float32)
    for k in range(1, column):
        column_copies[k - 1].wait_recv()
        start = start + to_here[k - 1] * totals_ref[k - 1]
    start_ref[y] = start
    start_copies = [
        remote(start_ref.at[y], start_ref.at[y], start_sems.at[k - 1], at_row(k)) for k in range(1, ROW)
    ]
    for k in farthest_first(ROW):
        start_copies[k - 1].start()
    for copy in start_copies:
        copy.wait_recv()

    for b in range(blocks):
        rows = slice(b * LANES, (b + 1) * LANES)
        incoming = through_row[b] * start_ref[b] + row_start[b]
        tall = jnp.broadcast_to(incoming[:, None, :], (ORDER, SUB, LANES)).reshape(LANES, LANES)
        spread = jnp.transpose(jnp.where(same, tall, 0.0))
        carried = dot_split(split(spread), split(readout_ref[rows, :]), NN)
        gated_ref[rows, :] = (query_ref[rows, :] * (base_ref[rows, :] + carried)).astype(jnp.bfloat16)

    loads[8].wait()
    gated = gated_ref[...]
    part = out_ref.shape[0]
    half = part // 2

    def share(k, whose):
        owner = wrapped(x + k, RING) * 2 + whose
        rows = pl.ds(pl.multiple_of(owner * part, part), part)
        return jnp.dot(out_weight_ref[rows, :], gated, preferred_element_type=jnp.float32)

    pair_copies = [remote(given_ref.at[k], pair_ref.at[k], pair_sems.at[k], partner) for k in range(RING)]
    top, bottom = pl.ds(0, half), pl.ds(half, half)
    relay_up = remote(mine_ref.at[2, top], relay_ref.at[0], ring_sems.at[0], at_ring(1))
    relay_down = remote(mine_ref.at[2, bottom], relay_ref.at[1], ring_sems.at[1], at_ring(-1))
    early_up = remote(mine_ref.at[1, bottom], last_ref.at[0, bottom], ring_sems.at[2], at_ring(1))
    early_down = remote(mine_ref.at[3, top], last_ref.at[1, top], ring_sems.at[3], at_ring(-1))
    late_up = remote(mine_ref.at[1, top], last_ref.at[0, top], ring_sems.at[4], at_ring(1))
    late_down = remote(mine_ref.at[3, bottom], last_ref.at[1, bottom], ring_sems.at[5], at_ring(-1))

    def offer(k):
        given_ref[k] = share(k, 1 - core)
        pair_copies[k].start()

    def meet(k):
        pair_copies[k].wait_recv()
        mine_ref[k] = mine_ref[k] + pair_ref[k]

    offer(2)
    offer(1)
    mine_ref[2] = share(2, core)
    offer(3)
    meet(2)
    relay_up.start()
    relay_down.start()
    mine_ref[1] = share(1, core)
    meet(1)
    early_up.start()
    mine_ref[3] = share(3, core)
    meet(3)
    early_down.start()
    offer(0)
    mine_ref[0] = share(0, core)
    meet(0)
    relay_up.wait_recv()
    mine_ref[1, top] = mine_ref[1, top] + relay_ref[0]
    late_up.start()
    relay_down.wait_recv()
    mine_ref[3, bottom] = mine_ref[3, bottom] + relay_ref[1]
    late_down.start()
    early_up.wait_recv()
    early_down.wait_recv()
    late_up.wait_recv()
    late_down.wait_recv()
    out_ref[...] = mine_ref[0] + last_ref[0] + last_ref[1]

    sent = halo_copies[0] + halo_copies[1] + halo_copies[2] + [extra_copy] + row_copies + column_copies + start_copies + pair_copies
    sent += [relay_up, relay_down, early_up, early_down, late_up, late_down]
    for copy in sent:
        copy.wait_send()


def per_device(features, short_filter, medium_filter, rates, residues, skip_gain, out_weight):
    channels, length = features.shape[1:]
    groups = rates.shape[0]
    blocks = channels // LANES
    column = lax.axis_size("seq") // ROW
    part = out_weight.shape[0] // lax.axis_size("tp")
    f32 = jnp.float32
    tile = (ORDER, LANES)
    half = jnp.bfloat16
    vmem = pl.BlockSpec(memory_space=pltpu.VMEM)
    hbm = pl.BlockSpec(memory_space=pltpu.HBM)
    pairs = lambda n: pltpu.SemaphoreType.DMA((n, 2))
    return pl.pallas_call(
        layer_kernel,
        out_shape=pltpu.VMEM((part, length), f32),
        in_specs=[hbm] * 7,
        out_specs=vmem,
        scratch_shapes=[
            pltpu.VMEM(features.shape, f32),
            pltpu.VMEM((3, SHORT, groups), f32),
            pltpu.VMEM(medium_filter.shape, f32),
            pltpu.VMEM((ORDER, groups), f32),
            pltpu.VMEM((ORDER, groups), f32),
            pltpu.VMEM((blocks, LANES), f32),
            pltpu.VMEM(out_weight.shape, half),
            pltpu.VMEM((blocks,) + tile, f32),
            pltpu.VMEM((2 * groups, 3 * LANES, LANES), half),
            pltpu.VMEM((2 * groups, 3 * LANES, LANES), half),
            pltpu.VMEM((groups, 2 * LANES, LANES), half),
            pltpu.VMEM((groups, 2 * LANES, LANES), half),
            pltpu.VMEM((3, channels, LANES), f32),
            pltpu.VMEM((3, 32, LANES), f32),
            pltpu.VMEM((3, 32, LANES), f32),
            pltpu.VMEM((3 * groups, length), f32),
            pltpu.VMEM((groups, length), f32),
            pltpu.VMEM((groups * ORDER, length), f32),
            pltpu.VMEM((groups * ORDER, length), f32),
            pltpu.VMEM((channels, length), f32),
            pltpu.VMEM((channels, length), f32),
            pltpu.VMEM((channels, length), f32),
            pltpu.VMEM((channels, length), half),
            pltpu.VMEM((blocks,) + tile, f32),
            pltpu.VMEM((ROW - 1, blocks) + tile, f32),
            pltpu.VMEM((blocks,) + tile, f32),
            pltpu.VMEM((column - 1,) + tile, f32),
            pltpu.VMEM((ROW,) + tile, f32),
            pltpu.VMEM((RING, part, length), f32),
            pltpu.VMEM((RING, part, length), f32),
            pltpu.VMEM((RING, part, length), f32),
            pltpu.VMEM((2, part // 2, length), f32),
            pltpu.VMEM((2, part, length), f32),
            pltpu.SemaphoreType.REGULAR((4,)),
            pltpu.SemaphoreType.DMA((9,)),
            pairs(3 * PARTS + 1), pairs(ROW - 1), pairs(column - 1), pairs(ROW - 1), pairs(RING), pairs(6),
        ],
        compiler_params=pltpu.CompilerParams(
            collective_id=0, has_side_effects=True, vmem_limit_bytes=58 * 1024 * 1024
        ),
    )(
        features, jnp.swapaxes(short_filter, 1, 2), medium_filter, rates.T, residues.T, skip_gain.reshape(blocks, LANES), out_weight,
    )


def solution(mesh):
    in_specs = (
        P(None, "tp", "seq"),
        P(None, "tp", None),
        P(None, "tp", None),
        P("tp", None),
        P("tp", None),
        P("tp"),
        P(None, "tp"),
    )
    out_specs = P("tp", "seq")
    return jax.shard_map(
        per_device, mesh=mesh, in_specs=in_specs, out_specs=out_specs, check_vma=False
    )
```

```python
import functools

import jax
import jax.numpy as jnp
from jax import lax
from jax.experimental import pallas as pl
from jax.experimental.pallas import tpu as pltpu
from jax.sharding import PartitionSpec as P

GROUP = 16
SHORT = 7
MEDIUM = 128
ORDER = 16
LANES = 128
ROW = 4
RING = 4
PARTS = 8
SUB = 8


def split(x):
    high = x.astype(jnp.bfloat16)
    return high, (x - high.astype(jnp.float32)).astype(jnp.bfloat16)


def dot_split(left, right, dims):
    a_high, a_low = left
    b_high, b_low = right
    one = functools.partial(
        lax.dot_general, dimension_numbers=(dims, ((), ())), preferred_element_type=jnp.float32
    )
    return one(a_high, b_high) + (one(a_high, b_low) + one(a_low, b_high))


NN = ((1,), (0,))
NT = ((1,), (1,))


def iota(shape, axis):
    return lax.broadcasted_iota(jnp.int32, shape, axis)


def upright(flat):
    rows, columns = flat.shape
    padded = jnp.concatenate([flat, jnp.zeros((rows, LANES - columns), jnp.float32)], axis=1)
    padded = jnp.concatenate([padded, jnp.zeros((LANES - rows, LANES), jnp.float32)], axis=0)
    return jnp.transpose(padded)[:columns]


def filter_tables(short_ref, medium_ref, taps_ref):
    branches, groups = medium_ref.shape[:2]
    for i in range(branches):
        medium, short = medium_ref[i], upright(short_ref[i])
        wide = jnp.concatenate([medium, jnp.zeros_like(medium)], axis=1)
        total = short[:, 0:1] * wide
        for j in range(1, SHORT):
            total = total + short[:, j : j + 1] * pltpu.roll(wide, j, 1)
        taps_ref[i * groups : (i + 1) * groups, :] = total


def one_less_decay(power):
    total = jnp.ones_like(power)
    for order in range(8, 1, -1):
        total = 1.0 - power * (1.0 / order) * total
    return power * total


def modal_tables(rates_ref, residues_ref, rate_blocks_ref, kernel_ref, ending_ref, readout_ref):
    groups, length = kernel_ref.shape
    steps = iota((1, length), 1).astype(jnp.float32)
    flat_rates = rates_ref[...]
    flat_weight = residues_ref[...] * jnp.sqrt(one_less_decay(2.0 * flat_rates))
    all_rates, all_weight = upright(flat_rates), upright(flat_weight)
    for b in range(groups // SUB):
        rates = all_rates[b * SUB : (b + 1) * SUB]
        weight = all_weight[b * SUB : (b + 1) * SUB]
        total = jnp.zeros((SUB, length), jnp.float32)
        for n in range(ORDER):
            rate, share = rates[:, n : n + 1], weight[:, n : n + 1]
            rows = slice((b * ORDER + n) * SUB, (b * ORDER + n + 1) * SUB)
            total = total + share * jnp.exp(-rate * steps)
            ending_ref[rows, :] = jnp.exp(-rate * (length - 1.0 - steps))
            readout_ref[rows, :] = share * jnp.exp(-rate * (steps + 1.0))
        kernel_ref[b * SUB : (b + 1) * SUB, :] = total
        wide = jnp.broadcast_to(rates[:, None, :], (SUB, GROUP, LANES)).reshape(SUB * GROUP, LANES)
        rate_blocks_ref[b] = jnp.transpose(wide)[:ORDER]


def toeplitz(row, rows):
    return pltpu.roll(jnp.broadcast_to(row, (rows, row.shape[1])), 0, 1, stride=1, stride_axis=0)


def filter_matrix(taps_row):
    rolled = toeplitz(taps_row, LANES)
    near, middle = rolled[:, :LANES], rolled[:, LANES:]
    causal = iota((LANES, LANES), 1) >= iota((LANES, LANES), 0)
    return split(jnp.concatenate(
        [jnp.where(causal, 0.0, near), middle, jnp.where(causal, near, 0.0)], axis=0
    ))


def long_matrix(row):
    rolled = toeplitz(row, LANES)
    near, middle = rolled[:, :LANES], rolled[:, LANES:]
    causal = iota((LANES, LANES), 1) >= iota((LANES, LANES), 0)
    return split(jnp.concatenate([middle, jnp.where(causal, near, 0.0)], axis=0))


def long_group(product, matrix):
    first, second = product[:, :LANES], product[:, LANES:]
    windows = jnp.concatenate(
        [jnp.concatenate([jnp.zeros_like(first), first], axis=1), product], axis=0
    )
    result = dot_split(split(windows), matrix, NN)
    return jnp.concatenate([result[:GROUP], result[GROUP:]], axis=1)


def filter_group(extra, halo, own, matrix):
    tiles = [extra, halo, own[:, :LANES], own[:, LANES:]]
    windows = jnp.concatenate(
        [jnp.concatenate(tiles[0:3], axis=1), jnp.concatenate(tiles[1:4], axis=1)], axis=0
    )
    result = dot_split(split(windows), matrix, NN)
    return jnp.concatenate([result[:GROUP], result[GROUP:]], axis=1)


def wrapped(index, count):
    return lax.rem(index + count, count)


def farthest_first(count):
    return sorted(range(1, count), key=lambda k: -min(k, count - k))


def layer_kernel(
    features_hbm, short_hbm, medium_hbm, rates_hbm, residues_hbm, gain_hbm, out_weight_hbm,
    out_ref,
    features_ref, short_ref, medium_ref, rates_ref, residues_ref, gain_ref, out_weight_ref, rate_blocks_ref,
    matrix_high_ref, matrix_low_ref, long_high_ref, long_low_ref,
    halo_ref, packed_ref, extra_ref, taps_ref, kernel_ref, ending_ref, readout_ref,
    product_ref, query_ref, base_ref, gated_ref,
    state_ref, row_states_ref, total_ref, totals_ref, start_ref,
    given_ref, mine_ref, pair_ref, relay_ref, last_ref,
    near_sems, local_sems,
    halo_sems, row_sems, column_sems, start_sems, pair_sems, ring_sems,
):
    groups, length = kernel_ref.shape
    channels = product_ref.shape[0]
    blocks = channels // LANES
    count = lax.axis_size("seq")
    column = count // ROW
    seq, tp = lax.axis_index("seq"), lax.axis_index("tp")
    z, y = seq // ROW, lax.rem(seq, ROW)
    x, core = tp // 2, lax.rem(tp, 2)
    at_row = lambda k: (z * ROW + wrapped(y + k, ROW), tp)
    at_column = lambda k: (wrapped(z + k, column) * ROW + y, tp)
    at_ring = lambda k: (seq, wrapped(x + k, RING) * 2 + core)
    following, before = (wrapped(seq + 1, count), tp), (wrapped(seq - 1, count), tp)
    partner = (seq, x * 2 + 1 - core)

    def signal(semaphore, device):
        pl.semaphore_signal(semaphore, inc=1, device_id=device, device_id_type=pl.DeviceIdType.MESH)

    def remote(source, target, sems, device):
        return pltpu.make_async_remote_copy(
            src_ref=source, dst_ref=target, send_sem=sems.at[0], recv_sem=sems.at[1],
            device_id=device, device_id_type=pl.DeviceIdType.MESH,
        )

    barrier = pltpu.get_barrier_semaphore()
    peers = [following, before, partner, at_ring(1), at_ring(-1)]
    peers += [at_row(1), at_row(-1), at_column(1), at_column(-1)]
    for peer in peers:
        signal(barrier, peer)
    whole = [short_hbm, medium_hbm, rates_hbm, residues_hbm, gain_hbm, out_weight_hbm]
    kept = [short_ref, medium_ref, rates_ref, residues_ref, gain_ref, out_weight_ref]
    loads = [pltpu.make_async_copy(features_hbm.at[i], features_ref.at[i], local_sems.at[i]) for i in range(3)]
    loads += [pltpu.make_async_copy(a, b, local_sems.at[3 + k]) for k, (a, b) in enumerate(zip(whole, kept))]
    for i in (1, 2, 0, 3, 4, 5, 6, 7, 8):
        loads[i].start()
    depth = channels // PARTS
    halo_copies = [
        [
            remote(
                features_hbm.at[i, pl.ds(b * depth, depth), pl.ds(length - LANES, LANES)],
                halo_ref.at[i, pl.ds(b * depth, depth)], halo_sems.at[i * PARTS + b], following,
            )
            for b in range(PARTS)
        ]
        for i in range(3)
    ]
    extra_copy = remote(packed_ref.at[pl.ds(1, 2)], extra_ref.at[pl.ds(1, 2)], halo_sems.at[3 * PARTS], following)
    extra_last = remote(packed_ref.at[0], extra_ref.at[0], halo_sems.at[3 * PARTS + 1], following)
    lane = iota((32, LANES), 1) // 8
    pl.semaphore_wait(barrier, len(peers))
    for b in range(2):
        halo_copies[1][b].start()
        halo_copies[2][b].start()
    for i in (1, 2, 0):
        loads[i].wait()
        packed = jnp.zeros((32, LANES), jnp.float32)
        for p in range(channels // 32):
            moved = pltpu.roll(features_ref[i, 32 * p : 32 * p + 32, 0:LANES], (8 * p + 8) % LANES, 1)
            packed = jnp.where(lane == p, moved, packed)
        packed_ref[i] = packed
        if i == 2:
            extra_copy.start()
    for b in range(2, PARTS):
        halo_copies[1][b].start()
        halo_copies[2][b].start()
    extra_last.start()
    for b in range(PARTS):
        halo_copies[0][b].start()

    signal(near_sems.at[3], at_row(1))
    signal(near_sems.at[3], at_row(-1))
    signal(near_sems.at[0], at_column(1))
    signal(near_sems.at[0], at_column(-1))
    for i in range(3, 8):
        loads[i].wait()
    filter_tables(short_ref, medium_ref, taps_ref)
    pl.semaphore_wait(near_sems.at[3], 2)
    pl.semaphore_wait(near_sems.at[0], 2)
    signal(near_sems.at[1], at_column(2))
    signal(near_sems.at[1], at_column(-2))
    modal_tables(rates_ref, residues_ref, rate_blocks_ref, kernel_ref, ending_ref, readout_ref)
    pl.semaphore_wait(near_sems.at[1], 2)
    signal(near_sems.at[2], at_column(4))
    signal(near_sems.at[2], at_column(-4))
    inner = seq > 0

    def matrices_step(half, carry):
        for g in [half * 2 + u for u in range(2)]:
            for i in (1, 2):
                place = (i - 1) * groups + g
                high, low = filter_matrix(taps_ref[pl.ds(i * groups + g, 1), :])
                matrix_high_ref[place] = high
                matrix_low_ref[place] = low
            high, low = long_matrix(kernel_ref[pl.ds(g, 1), :])
            long_high_ref[g] = high
            long_low_ref[g] = low
        return carry

    def branch(i, g, matrix):
        rows = pl.ds(pl.multiple_of(g * GROUP, GROUP), GROUP)
        packed = extra_ref[i, pl.ds(pl.multiple_of(lax.rem(g, 2) * GROUP, GROUP), GROUP), :]
        extra = pltpu.roll(packed, LANES - 8 - 8 * (g // 2), 1)
        zero = jnp.zeros((GROUP, LANES), jnp.float32)
        return filter_group(
            jnp.where(inner, extra, zero), jnp.where(inner, halo_ref[i, rows, :], zero),
            features_ref[i, rows, :], matrix,
        )

    def product_step(half, carry):
        for g in [half * 4 + u for u in range(4)]:
            rows = pl.ds(pl.multiple_of(g * GROUP, GROUP), GROUP)
            key = branch(1, g, (matrix_high_ref[g], matrix_low_ref[g]))
            value = branch(2, g, (matrix_high_ref[groups + g], matrix_low_ref[groups + g]))
            product = key * value
            product_ref[rows, :] = product
        return carry

    def base_step(half, carry):
        for g in [half * 4 + u for u in range(4)]:
            rows = pl.ds(pl.multiple_of(g * GROUP, GROUP), GROUP)
            base_ref[rows, :] = long_group(product_ref[rows, :], (long_high_ref[g], long_low_ref[g]))
        return carry

    def query_step(half, carry):
        for g in [half * 2 + u for u in range(2)]:
            rows = pl.ds(pl.multiple_of(g * GROUP, GROUP), GROUP)
            query_ref[rows, :] = branch(0, g, filter_matrix(taps_ref[pl.ds(g, 1), :]))
        return carry

    lax.fori_loop(0, groups // 2, matrices_step, 0)
    pl.semaphore_wait(near_sems.at[2], 2)
    extra_copy.wait_recv()
    same = lax.rem(iota((LANES, LANES), 0), SUB) == iota((LANES, LANES), 1) // GROUP
    part_steps = groups // PARTS // 4
    for b in range(blocks):
        for p in range(b * PARTS // blocks, (b + 1) * PARTS // blocks):
            halo_copies[1][p].wait_recv()
            halo_copies[2][p].wait_recv()
            lax.fori_loop(p * part_steps, (p + 1) * part_steps, product_step, 0)
        rows = slice(b * LANES, (b + 1) * LANES)
        full = dot_split(split(ending_ref[rows, :]), split(product_ref[rows, :]), NT)
        full = jnp.where(same, full, 0.0)
        state_ref[b] = jnp.sum(full.reshape(ORDER, SUB, LANES), axis=1)
    row_copies = [
        remote(state_ref, row_states_ref.at[k - 1], row_sems.at[k - 1], at_row(k)) for k in range(1, ROW)
    ]
    for k in farthest_first(ROW):
        row_copies[k - 1].start()
    lax.fori_loop(0, groups // 8, base_step, 0)

    rates = rate_blocks_ref[...]
    decay = lambda rates, steps: jnp.exp(-rates * (float(length) * steps))
    as_float = lambda value: lax.convert_element_type(value, jnp.float32)
    to_total = [decay(rates, as_float(ROW - 1 - wrapped(y - k, ROW))) for k in range(ROW)]
    to_start = [jnp.where(k <= y, decay(rates, k - 1.0), 0.0) for k in range(1, ROW)]
    row_start = jnp.zeros(rates.shape, jnp.float32)
    row_total = to_total[0] * state_ref[...]
    for k in range(1, ROW):
        row_copies[k - 1].wait_recv()
        state = row_states_ref[k - 1]
        row_start = row_start + to_start[k - 1] * state
        row_total = row_total + to_total[k] * state
    total_ref[...] = row_total
    column_copies = [
        remote(total_ref.at[y], totals_ref.at[k - 1], column_sems.at[k - 1], at_column(k))
        for k in range(1, column)
    ]
    for k in farthest_first(column):
        column_copies[k - 1].start()

    for copy in halo_copies[0]:
        copy.wait_recv()
    extra_last.wait_recv()
    lax.fori_loop(0, groups // 2, query_step, 0)
    lax.fori_loop(groups // 8, groups // 4, base_step, 0)
    for b in range(blocks):
        rows = slice(b * LANES, (b + 1) * LANES)
        gain = jnp.transpose(jnp.broadcast_to(gain_ref[b : b + 1, :], (LANES, LANES)))
        base_ref[rows, :] = base_ref[rows, :] + jnp.concatenate([gain] * (length // LANES), axis=1) * product_ref[rows, :]

    quarter = rate_blocks_ref[y]
    to_here = [
        jnp.where(k <= z, decay(quarter, float(ROW * (k - 1))), 0.0) for k in range(1, column)
    ]
    through_row = decay(rates, as_float(y))
    start = jnp.zeros(quarter.shape, jnp.float32)
    for k in range(1, column):
        column_copies[k - 1].wait_recv()
        start = start + to_here[k - 1] * totals_ref[k - 1]
    start_ref[y] = start
    start_copies = [
        remote(start_ref.at[y], start_ref.at[y], start_sems.at[k - 1], at_row(k)) for k in range(1, ROW)
    ]
    for k in farthest_first(ROW):
        start_copies[k - 1].start()
    for copy in start_copies:
        copy.wait_recv()

    for b in range(blocks):
        rows = slice(b * LANES, (b + 1) * LANES)
        incoming = through_row[b] * start_ref[b] + row_start[b]
        tall = jnp.broadcast_to(incoming[:, None, :], (ORDER, SUB, LANES)).reshape(LANES, LANES)
        spread = jnp.transpose(jnp.where(same, tall, 0.0))
        carried = dot_split(split(spread), split(readout_ref[rows, :]), NN)
        gated_ref[rows, :] = (query_ref[rows, :] * (base_ref[rows, :] + carried)).astype(jnp.bfloat16)

    loads[8].wait()
    gated = gated_ref[...]
    part = out_ref.shape[0]
    half = part // 2

    def share(k, whose):
        owner = wrapped(x + k, RING) * 2 + whose
        rows = pl.ds(pl.multiple_of(owner * part, part), part)
        return jnp.dot(out_weight_ref[rows, :], gated, preferred_element_type=jnp.float32)

    pair_copies = [remote(given_ref.at[k], pair_ref.at[k], pair_sems.at[k], partner) for k in range(RING)]
    top, bottom = pl.ds(0, half), pl.ds(half, half)
    relay_up = remote(mine_ref.at[2, top], relay_ref.at[0], ring_sems.at[0], at_ring(1))
    relay_down = remote(mine_ref.at[2, bottom], relay_ref.at[1], ring_sems.at[1], at_ring(-1))
    early_up = remote(mine_ref.at[1, bottom], last_ref.at[0, bottom], ring_sems.at[2], at_ring(1))
    early_down = remote(mine_ref.at[3, top], last_ref.at[1, top], ring_sems.at[3], at_ring(-1))
    late_up = remote(mine_ref.at[1, top], last_ref.at[0, top], ring_sems.at[4], at_ring(1))
    late_down = remote(mine_ref.at[3, bottom], last_ref.at[1, bottom], ring_sems.at[5], at_ring(-1))

    def offer(k):
        given_ref[k] = share(k, 1 - core)
        pair_copies[k].start()

    def meet(k):
        pair_copies[k].wait_recv()
        mine_ref[k] = mine_ref[k] + pair_ref[k]

    offer(2)
    offer(1)
    mine_ref[2] = share(2, core)
    offer(3)
    meet(2)
    relay_up.start()
    relay_down.start()
    mine_ref[1] = share(1, core)
    meet(1)
    early_up.start()
    mine_ref[3] = share(3, core)
    meet(3)
    early_down.start()
    offer(0)
    mine_ref[0] = share(0, core)
    meet(0)
    relay_up.wait_recv()
    mine_ref[1, top] = mine_ref[1, top] + relay_ref[0]
    late_up.start()
    relay_down.wait_recv()
    mine_ref[3, bottom] = mine_ref[3, bottom] + relay_ref[1]
    late_down.start()
    early_up.wait_recv()
    early_down.wait_recv()
    late_up.wait_recv()
    late_down.wait_recv()
    out_ref[...] = mine_ref[0] + last_ref[0] + last_ref[1]

    sent = halo_copies[0] + halo_copies[1] + halo_copies[2] + [extra_copy, extra_last] + row_copies + column_copies + start_copies + pair_copies
    sent += [relay_up, relay_down, early_up, early_down, late_up, late_down]
    for copy in sent:
        copy.wait_send()


def per_device(features, short_filter, medium_filter, rates, residues, skip_gain, out_weight):
    channels, length = features.shape[1:]
    groups = rates.shape[0]
    blocks = channels // LANES
    column = lax.axis_size("seq") // ROW
    part = out_weight.shape[0] // lax.axis_size("tp")
    f32 = jnp.float32
    tile = (ORDER, LANES)
    half = jnp.bfloat16
    vmem = pl.BlockSpec(memory_space=pltpu.VMEM)
    hbm = pl.BlockSpec(memory_space=pltpu.HBM)
    pairs = lambda n: pltpu.SemaphoreType.DMA((n, 2))
    return pl.pallas_call(
        layer_kernel,
        out_shape=pltpu.VMEM((part, length), f32),
        in_specs=[hbm] * 7,
        out_specs=vmem,
        scratch_shapes=[
            pltpu.VMEM(features.shape, f32),
            pltpu.VMEM((3, SHORT, groups), f32),
            pltpu.VMEM(medium_filter.shape, f32),
            pltpu.VMEM((ORDER, groups), f32),
            pltpu.VMEM((ORDER, groups), f32),
            pltpu.VMEM((blocks, LANES), f32),
            pltpu.VMEM(out_weight.shape, half),
            pltpu.VMEM((blocks,) + tile, f32),
            pltpu.VMEM((2 * groups, 3 * LANES, LANES), half),
            pltpu.VMEM((2 * groups, 3 * LANES, LANES), half),
            pltpu.VMEM((groups, 2 * LANES, LANES), half),
            pltpu.VMEM((groups, 2 * LANES, LANES), half),
            pltpu.VMEM((3, channels, LANES), f32),
            pltpu.VMEM((3, 32, LANES), f32),
            pltpu.VMEM((3, 32, LANES), f32),
            pltpu.VMEM((3 * groups, length), f32),
            pltpu.VMEM((groups, length), f32),
            pltpu.VMEM((groups * ORDER, length), f32),
            pltpu.VMEM((groups * ORDER, length), f32),
            pltpu.VMEM((channels, length), f32),
            pltpu.VMEM((channels, length), f32),
            pltpu.VMEM((channels, length), f32),
            pltpu.VMEM((channels, length), half),
            pltpu.VMEM((blocks,) + tile, f32),
            pltpu.VMEM((ROW - 1, blocks) + tile, f32),
            pltpu.VMEM((blocks,) + tile, f32),
            pltpu.VMEM((column - 1,) + tile, f32),
            pltpu.VMEM((ROW,) + tile, f32),
            pltpu.VMEM((RING, part, length), f32),
            pltpu.VMEM((RING, part, length), f32),
            pltpu.VMEM((RING, part, length), f32),
            pltpu.VMEM((2, part // 2, length), f32),
            pltpu.VMEM((2, part, length), f32),
            pltpu.SemaphoreType.REGULAR((4,)),
            pltpu.SemaphoreType.DMA((9,)),
            pairs(3 * PARTS + 2), pairs(ROW - 1), pairs(column - 1), pairs(ROW - 1), pairs(RING), pairs(6),
        ],
        compiler_params=pltpu.CompilerParams(
            collective_id=0, has_side_effects=True, vmem_limit_bytes=58 * 1024 * 1024
        ),
    )(
        features, jnp.swapaxes(short_filter, 1, 2), medium_filter, rates.T, residues.T, skip_gain.reshape(blocks, LANES), out_weight,
    )


def solution(mesh):
    in_specs = (
        P(None, "tp", "seq"),
        P(None, "tp", None),
        P(None, "tp", None),
        P("tp", None),
        P("tp", None),
        P("tp"),
        P(None, "tp"),
    )
    out_specs = P("tp", "seq")
    return jax.shard_map(
        per_device, mesh=mesh, in_specs=in_specs, out_specs=out_specs, check_vma=False
    )
```
